32 devices in a mesh: mkt: 8 (over z, y), draw: 4 (over x, core).
Axes of the slice: x: 2, y: 2, z: 4, core: 2. Of those that a mesh axis runs over, the one named last changes fastest.
Arguments:
- x_char: float32 [384, 56, 8], P('mkt'), may hold values from -2.5 to 2.5
- nu_draws: float32 [384, 8, 2048], P('mkt', None, 'draw'), may hold values from -3 to 3
- coef_sigma: float32 [8], replicated, may hold values from 0.3 to 1.2
- log_share: float32 [384, 56], P('mkt'), may hold values from -7 to -4.5
- counts: int32 [384], P('mkt'), may hold values from 28 to 56
Outputs:
- mean_util: float32 [384, 56], P('mkt')
- jacobian: float32 [384, 56, 56], P(('mkt', 'draw'))
- sup_norms: float32 [3], replicated
The draws below stay inside these ranges and needn't reach their ends.
Inputs may be any that keep to these rules, and one draw needn't show every extreme that they name: Products 0 to counts - 1 of a market are valid; the other slots are padding.
All inputs are finite; a program needn't handle non-finite values. Where the reference program divides by a largest or mean magnitude, that divisor is 1e-20 or more.
Results may differ from the reference program's by a relative error of at most 0.00013.
Values sent between devices are 32-bit elements; how exact they have to be, the bound alone decides.
A program may use at most 64 MiB of HBM per device.

```python
import math
import jax
import jax.numpy as jnp
from jax import lax

J = 56
K = 8
ITERS = 3
M = 384
R = 2048


def set_ends(array, key, least, top_value):
    longest = array.shape.index(max(array.shape))
    spots = []
    for shift in (0, 1):
        where = [jax.random.randint(jax.random.fold_in(key, axis), (), 0, length) for axis, length in enumerate(array.shape)]
        where[longest] = (where[longest] + shift) % array.shape[longest]
        spots.append(tuple(where))
    return array.at[spots[0]].set(least).at[spots[1]].set(top_value)


def shard_levels(key, shape, pieces, least, top_value):
    gain, own = 1.0, jax.random.fold_in(key, 6)
    for position, blocks in pieces:
        heights = jnp.exp(jax.random.uniform(jax.random.fold_in(own, position), (blocks,), jnp.float32, least / len(pieces), top_value / len(pieces)))
        gain = gain * jnp.repeat(heights, shape[position] // blocks).reshape([-1 if axis == position else 1 for axis in range(len(shape))])
    return gain


def gaussian(key, shape, spread, bound, cuts=(), kind=jnp.bfloat16):
    array = spread * jax.random.normal(key, shape, jnp.float32)
    if cuts:
        array = array * shard_levels(key, shape, cuts, -0.22, 0.18)
    return jnp.clip(array, -bound, bound).astype(kind)


def setup_inputs(seed: int = 0) -> dict:
    seeds = jax.random.split(jax.random.key(seed), 6)
    return {
        "x_char": gaussian(seeds[0], (M, J, K), 1.0, 2.5, ((0, 8),), jnp.float32),
        "nu_draws": gaussian(seeds[1], (M, K, R), 1.0, 3.0, ((0, 8), (2, 4)), jnp.float32),
        "coef_sigma": jnp.clip(jnp.exp(jax.random.uniform(seeds[2], (K,), jnp.float32, math.log(0.3), math.log(1.2))), 0.3, 1.2),
        "log_share": jnp.clip(-7.0 + 2.5 * jax.random.uniform(seeds[3], (M, J), jnp.float32) ** shard_levels(seeds[3], (M, J), ((0, 8),), -0.2, 0.2), -7.0, -4.5),
        "counts": set_ends(jax.random.randint(seeds[4], (M,), J // 2, J + 1), jax.random.fold_in(seeds[4], 1), J // 2, J).astype(jnp.int32),
    }


step_cap = 0.25
epsilon = 1e-6


def market_terms(mean_util, scaled, nu_draws, usable, inverse, with_products):
    tastes = jnp.einsum("mjk,mkr->mjr", scaled, nu_draws, precision=lax.Precision.HIGHEST)
    raised = jnp.where(usable[:, :, None], jnp.exp(mean_util[:, :, None] + tastes), 0.0)
    chance = raised / (1.0 + jnp.sum(raised, axis=1, keepdims=True))
    shares = jnp.sum(chance, axis=2) * inverse
    if with_products:
        cross_sums = jnp.einsum("mjr,mlr->mjl", chance, chance, precision=lax.Precision.HIGHEST) * inverse
        return shares, cross_sums
    return shares


def evaluate(mean_util, scaled, nu_draws, usable, inverse, with_products):
    groups = mean_util.shape[0] // 8
    folded = (mean_util.reshape(groups, 8, mean_util.shape[1]),
              scaled.reshape(groups, 8, scaled.shape[1], scaled.shape[2]),
              nu_draws.reshape(groups, 8, nu_draws.shape[1], nu_draws.shape[2]),
              usable.reshape(groups, 8, usable.shape[1]))

    def per_group(items):
        return market_terms(items[0], items[1], items[2], items[3], inverse, with_products)

    def unfold(member):
        return member.reshape((groups * 8,) + member.shape[2:])

    return jax.tree.map(unfold, lax.map(per_group, folded))


def reference(x_char, nu_draws, coef_sigma, log_share, counts):
    usable = jnp.arange(J, dtype=jnp.int32)[None, :] < counts[:, None]
    scaled = x_char * coef_sigma[None, None, :]
    inverse = 1.0 / R
    inside = jnp.sum(jnp.where(usable, jnp.exp(log_share), 0.0), axis=1)
    mean_util = jnp.where(usable, log_share - jnp.log(1.0 - inside)[:, None], 0.0)
    norms_list = []
    for sweep in range(ITERS):
        shares = evaluate(mean_util, scaled, nu_draws, usable, inverse, False)
        change = jnp.where(usable, log_share - jnp.log(jnp.where(usable, shares, 1.0)), 0.0)
        largest = jnp.max(jnp.abs(change))
        mean_util = mean_util + jnp.minimum(1.0, step_cap / (largest + epsilon)) * change
        norms_list.append(largest)
    shares, cross_sums = evaluate(mean_util, scaled, nu_draws, usable, inverse, True)
    divisor = jnp.where(usable, shares, 1.0)
    identity = jnp.eye(J, dtype=jnp.float32)
    paired = usable[:, :, None] & usable[:, None, :]
    jacobian = jnp.where(paired, identity[None, :, :] - cross_sums / divisor[:, :, None], 0.0)
    return mean_util, jacobian, jnp.stack(norms_list)
```

```python
import functools
import math

import jax
import jax.numpy as jnp
from jax import lax
from jax.experimental import pallas as pl
from jax.experimental.pallas import tpu as pltpu
from jax.sharding import PartitionSpec as P

ITERS = 3
LANES = 128
BLOCK = 4
PIECES = 4
EARLY = 1
VMEM_LIMIT = 48 * 1024 * 1024
MESH = pl.DeviceIdType.MESH

step_cap = 0.25
epsilon = 1e-06


def divisor_up_to(count, most):
    return max(size for size in range(1, most + 1) if count % size == 0)


def rounded(value):
    return value.astype(jnp.bfloat16).astype(jnp.float32)


def split2(value):
    first = rounded(value)
    return first, value - first


def kernel(
    draws,
    chips,
    inverse,
    sigma_hbm,
    counts_hbm,
    counts_row_hbm,
    log_share_hbm,
    x_hbm,
    nu_hbm,
    mean_out,
    jac_out,
    norms_out,
    sigma_ref,
    counts_ref,
    counts_row_ref,
    log_share_ref,
    x_ref,
    nu_ref,
    far_ref,
    held,
    first_ref,
    inverse_ref,
    rows_ref,
    square,
    turn,
    part_slots,
    peak_slots,
    peaks_slots,
    mean_slots,
    part_send_sem,
    part_recv_sem,
    peak_send_sem,
    peak_recv_sem,
    peaks_send_sem,
    peaks_recv_sem,
    far_send_sem,
    far_recv_sem,
    mean_send_sem,
    mean_recv_sem,
    load_sem,
    nu_sem,
):
    markets, coefs, slots = x_ref.shape
    own = markets // draws
    consumers = nu_ref.shape[3]
    tiles = slots // 8
    half = LANES // 2
    block = inverse_ref.shape[0]
    pieces = far_send_sem.shape[1]
    piece = own // pieces
    my_draw = lax.axis_index("draw")
    my_mkt = lax.axis_index("mkt")
    cores = 2 if draws % 2 == 0 else 1

    def partner(k):
        chip = (my_draw // cores + (k - 1) // cores + 1) % (draws // cores)
        core = (my_draw + k) % cores
        return chip * cores + core

    loads = [
        pltpu.make_async_copy(source, target, load_sem.at[n])
        for n, (source, target) in enumerate(
            (
                (counts_row_hbm, counts_row_ref),
                (log_share_hbm, log_share_ref),
                (sigma_hbm, sigma_ref),
                (counts_hbm, counts_ref),
                (x_hbm, x_ref),
            )
        )
    ]

    def nu_load(k):
        return pltpu.make_async_copy(
            nu_hbm.at[pl.ds(partner(k) * own, own)], nu_ref.at[k - 1], nu_sem.at[k - 1]
        )

    for load in loads:
        load.start()
    for k in range(1, draws + 1):
        nu_load(k).start()

    barrier = pltpu.get_barrier_semaphore()
    for k in range(1, draws):
        pl.semaphore_signal(
            barrier, inc=1, device_id={"draw": lax.rem(my_draw + k, draws)}, device_id_type=MESH
        )
    for k in range(1, chips):
        pl.semaphore_signal(
            barrier, inc=1, device_id={"mkt": lax.rem(my_mkt + k, chips)}, device_id_type=MESH
        )

    def far_copy(k, c):
        return pltpu.make_async_remote_copy(
            src_ref=nu_hbm.at[pl.ds(partner(k) * own + c * piece, piece)],
            dst_ref=far_ref.at[k - 1, pl.ds(c * piece, piece)],
            send_sem=far_send_sem.at[k - 1, c],
            recv_sem=far_recv_sem.at[k - 1, c],
            device_id={"draw": partner(k)},
            device_id_type=MESH,
        )

    near = range(max(1, draws - cores + 1), draws)
    distant = range(1, max(1, draws - cores + 1))

    lane = lax.broadcasted_iota(jnp.int32, (slots, LANES), 1)
    row = lax.broadcasted_iota(jnp.int32, (slots, LANES), 0)
    lane8 = lax.broadcasted_iota(jnp.int32, (8, LANES), 1)
    row8 = lax.broadcasted_iota(jnp.int32, (8, LANES), 0)

    square[...] = jnp.zeros_like(square)
    for load in loads:
        load.wait()
    square[0:markets, 0:slots] = log_share_ref[...]
    log_share = square[...].T[0:slots, :]
    square[0:1, 0:markets] = counts_row_ref[...].astype(jnp.float32)
    counts = square[0:1, :]
    usable = (row.astype(jnp.float32) < counts) & (lane < markets)
    inside = jnp.sum(jnp.where(usable, jnp.exp(log_share), 0.0), axis=0, keepdims=True)
    mean = jnp.where(usable, log_share - jnp.log(1.0 - inside), 0.0)
    weights = jnp.where(usable, jnp.exp(mean), 0.0)

    coef_row = lax.broadcasted_iota(jnp.int32, (coefs, slots), 0)
    sigma = jnp.zeros((coefs, slots), jnp.float32)
    for k in range(coefs):
        sigma = jnp.where(coef_row == k, sigma_ref[k] * math.log2(math.e), sigma)

    def raised_tastes(chars, draw):
        s1, s2 = split2(chars * sigma)
        n1, n2 = split2(draw)
        left = jnp.concatenate([s1, s1, s2, s2], axis=0).astype(jnp.bfloat16)
        right = jnp.concatenate([n1, n2, n1, n2], axis=0).astype(jnp.bfloat16)
        tastes = lax.dot_general(
            left, right, (((0,), (0,)), ((), ())), preferred_element_type=jnp.float32
        )
        return jnp.exp2(tastes)

    def packed(value, base):
        total = jnp.zeros((8, LANES), jnp.float32)
        for t in range(tiles):
            shift = (t * own - base) % LANES
            moved = value[8 * t : 8 * t + 8]
            moved = pltpu.roll(moved, shift, 1) if shift else moved
            total = jnp.where((lane8 >= t * own) & (lane8 < (t + 1) * own), moved, total)
        return total

    def unpacked(value):
        return jnp.concatenate(
            [pltpu.roll(value, LANES - t * own, 1) if t else value for t in range(tiles)], axis=0
        )

    def placed(part, column, i):
        for t in range(tiles):
            part = jnp.where(lane8 == t * own + i, column[8 * t : 8 * t + 8], part)
        return part

    pl.semaphore_wait(barrier, draws - 1 + chips - 1)
    for k in near:
        for c in range(pieces):
            far_copy(k, c).start()
    for c in range(min(EARLY, pieces)):
        for k in distant:
            far_copy(k, c).start()

    def part_copy(k, g):
        return pltpu.make_async_remote_copy(
            src_ref=part_slots.at[my_draw, partner(g)],
            dst_ref=part_slots.at[my_draw, partner(g)],
            send_sem=part_send_sem.at[k - 1, g - 1],
            recv_sem=part_recv_sem.at[k - 1, g - 1],
            device_id={"draw": lax.rem(my_draw + k, draws)},
            device_id_type=MESH,
        )

    mine = (draws - 1) * consumers
    near_chunks = [
        slice(at, min(at + LANES, consumers)) for at in range(0, consumers, LANES)
    ]

    def first_sweep(g, carry):
        base = partner(g) * own
        nu_load(g).wait()
        local = pltpu.roll(weights, lax.rem(LANES - base, LANES), 1)
        for i in range(own):
            weight = local[:, i : i + 1]
            known = raised_tastes(x_ref[base + i], nu_ref[g - 1, i])
            held[i, :, mine : mine + consumers] = known
            for chunk in near_chunks:
                first_ref[i : i + 1, chunk] = 1.0 + jnp.sum(
                    weight * known[:, chunk], axis=0, keepdims=True
                )
        first_ref[...] = 1.0 / first_ref[...]
        part = jnp.zeros((8, LANES), jnp.float32)
        for i in range(own):
            column = None
            for chunk in near_chunks:
                term = (
                    held[i, :, mine + chunk.start : mine + chunk.stop]
                    * first_ref[i : i + 1, chunk]
                )
                column = term if column is None else column + term
            part = placed(part, jnp.sum(column, axis=1, keepdims=True), i)
        part_slots[my_draw, partner(g)] = part
        for k in range(1, draws):
            part_copy(k, g).start()
        return carry

    lax.fori_loop(1, draws + 1, first_sweep, 0)

    for c in range(min(EARLY, pieces), pieces):
        for k in distant:
            far_copy(k, c).start()

    def fill(k, c):
        far_copy(k, c).wait_recv()

        def body(i, carry):
            m = c * piece + i
            held[m, :, (k - 1) * consumers : k * consumers] = raised_tastes(
                x_ref[my_draw * own + m], far_ref[k - 1, m]
            )
            return carry

        lax.fori_loop(0, piece, body, 0, unroll=True)

    for c in range(pieces):
        for k in near:
            fill(k, c)

    product = row8
    for t in range(1, tiles):
        product = jnp.where(lane8 >= t * own, row8 + 8 * t, product)
    wide_counts = jnp.broadcast_to(counts, (slots, LANES))
    ls, means, valid = [], [], []
    for g in range(draws):
        ls.append(packed(log_share, g * own))
        means.append(packed(mean, g * own))
        valid.append(
            (product.astype(jnp.float32) < packed(wide_counts, g * own)) & (lane8 < tiles * own)
        )

    def change_of(weight, total, ls, valid):
        shares = jnp.where(valid, weight * total * inverse, 1.0)
        return jnp.where(valid, ls - jnp.log(shares), 0.0)

    start_weights = [jnp.where(valid[g], jnp.exp(means[g]), 0.0) for g in range(draws)]
    for g in range(1, draws + 1):
        for k in range(1, draws):
            part_copy(k, g).wait_recv()
    changes = []
    peak = jnp.zeros((8, LANES), jnp.float32)
    for g in range(draws):
        total = part_slots[0, g]
        for d in range(1, draws):
            total = total + part_slots[d, g]
        changes.append(change_of(start_weights[g], total, ls[g], valid[g]))
        peak = jnp.maximum(peak, jnp.abs(changes[g]))
    peak_slots[0] = jnp.max(peak, axis=0, keepdims=True)

    def peak_copy(k):
        return pltpu.make_async_remote_copy(
            src_ref=peak_slots.at[0],
            dst_ref=peak_slots.at[k],
            send_sem=peak_send_sem.at[k - 1],
            recv_sem=peak_recv_sem.at[k - 1],
            device_id={"mkt": lax.rem(my_mkt + k, chips)},
            device_id_type=MESH,
        )

    for k in range(1, chips):
        peak_copy(k).start()

    def choose(values):
        chosen = values[0]
        for g in range(1, draws):
            chosen = jnp.where(my_draw == g, values[g], chosen)
        return chosen

    ls_own = choose(ls)
    mean_own = choose(means)
    change = choose(changes)
    count_own = choose([packed(wide_counts, g * own) for g in range(draws)])
    valid_own = (product.astype(jnp.float32) < count_own) & (lane8 < tiles * own)

    for c in range(pieces):
        for k in distant:
            fill(k, c)

    def largest_of(slots_ref):
        rows = [slots_ref[n] for n in range(slots_ref.shape[0])]
        while len(rows) > 1:
            rows = [
                jnp.maximum(rows[n], rows[n + 1]) if n + 1 < len(rows) else rows[n]
                for n in range(0, len(rows), 2)
            ]
        return jnp.max(rows[0], axis=1, keepdims=True)

    def step_of(largest):
        return jnp.minimum(1.0, step_cap / (largest + epsilon))

    for k in range(1, chips):
        peak_copy(k).wait_recv()
    norms = [largest_of(peak_slots)]
    mean_own = mean_own + step_of(norms[0]) * change

    lanes_of = [slice(at, at + LANES) for at in range(0, draws * consumers, LANES)]

    def denominators(local, b):
        for u in range(block):
            weight = jnp.concatenate(
                [local[:, t * own + u : t * own + u + 1] for t in range(tiles)], axis=0
            )
            for n, chunk in enumerate(lanes_of):
                inverse_ref[u, n : n + 1, :] = 1.0 + jnp.sum(
                    weight * held[b * block + u, :, chunk], axis=0, keepdims=True
                )
        inverse_ref[...] = 1.0 / inverse_ref[...]

    def sweep(weight):
        def body(b, part):
            local = pltpu.roll(weight, lax.rem(LANES - b * block, LANES), 1)
            denominators(local, b)
            for u in range(block):
                column = None
                for n, chunk in enumerate(lanes_of):
                    term = held[b * block + u, :, chunk] * inverse_ref[u, n : n + 1, :]
                    column = term if column is None else column + term
                part = placed(part, jnp.sum(column, axis=1, keepdims=True), b * block + u)
            return part

        return lax.fori_loop(0, own // block, body, jnp.zeros((8, LANES), jnp.float32))

    others = [(m, d) for m in range(chips) for d in range(draws) if m or d]

    def peaks_copy(it, n):
        m, d = others[n]
        return pltpu.make_async_remote_copy(
            src_ref=peaks_slots.at[it, 0],
            dst_ref=peaks_slots.at[it, n + 1],
            send_sem=peaks_send_sem.at[it],
            recv_sem=peaks_recv_sem.at[it],
            device_id={
                "mkt": lax.rem(my_mkt + m, chips),
                "draw": lax.rem(my_draw + d, draws),
            },
            device_id_type=MESH,
        )

    def peaks_all(it, sem):
        span = peaks_slots.at[it, pl.ds(1, len(others))]
        return pltpu.make_async_copy(span, span, sem.at[it])

    for it in range(ITERS - 1):
        weight = jnp.where(valid_own, jnp.exp(mean_own), 0.0)
        change = change_of(weight, sweep(weight), ls_own, valid_own)
        peaks_slots[it, 0] = jnp.max(jnp.abs(change), axis=0, keepdims=True)
        for n in range(len(others)):
            peaks_copy(it, n).start()
        peaks_all(it, peaks_recv_sem).wait()
        norms.append(largest_of(peaks_slots.at[it]))
        mean_own = mean_own + step_of(norms[-1]) * change

    square[0:slots, :] = unpacked(mean_own)
    mean_rows = square[...].T[0:own, :]
    mean_slots[my_draw] = mean_rows
    rows_ref[...] = jnp.exp(mean_rows)

    def mean_copy(k):
        return pltpu.make_async_remote_copy(
            src_ref=mean_slots.at[my_draw],
            dst_ref=mean_slots.at[my_draw],
            send_sem=mean_send_sem.at[k - 1],
            recv_sem=mean_recv_sem.at[k - 1],
            device_id={"draw": lax.rem(my_draw + k, draws)},
            device_id_type=MESH,
        )

    for k in range(1, draws):
        mean_copy(k).start()

    weight = jnp.where(valid_own, jnp.exp(mean_own), 0.0)
    eye = jnp.where(row == lane, 1.0, 0.0)
    ones = jnp.ones((8, draws * consumers), jnp.float32)
    scale = jnp.where(lax.broadcasted_iota(jnp.int32, (half, LANES), 0) < slots, 0.5, 1.0)
    low_half = lax.broadcasted_iota(jnp.int32, (half, LANES), 1) < half

    def last_sweep(b, carry):
        local = pltpu.roll(weight, lax.rem(LANES - b * block, LANES), 1)
        denominators(local, b)
        sums = []
        for u in range(block):
            chance = jnp.concatenate(
                [
                    held[b * block + u, :, chunk] * inverse_ref[u, n : n + 1, :]
                    for n, chunk in enumerate(lanes_of)
                ],
                axis=1,
            )
            low = chance - rounded(chance)
            left = jnp.concatenate([chance, ones], axis=0).astype(jnp.bfloat16)
            right = jnp.concatenate([chance, low], axis=0).astype(jnp.bfloat16)
            products = lax.dot_general(
                left, right, (((1,), (1,)), ((), ())), preferred_element_type=jnp.float32
            )
            products = jnp.concatenate(
                [products, jnp.zeros((half, LANES - 2 * slots), jnp.float32)], axis=1
            )
            sums.append(scale * products + pltpu.roll(products, LANES - slots, 1))
        for at in range(0, block, 2):
            pair = sums[at]
            if at + 1 < block:
                pair = jnp.where(low_half, pair, pltpu.roll(sums[at + 1], half, 1))
            turn[at // 2 * half : at // 2 * half + half, :] = pair
        turn[...] = turn[...].T
        for u in range(block):
            other = turn[u % 2 * half : u % 2 * half + slots, :]
            other = pltpu.roll(other, half, 1) if u // 2 else other
            m = b * block + u
            count = counts_ref[my_draw * own + m]
            here = (row < count) & (lane < count)
            ratio = (sums[u][0:slots] + other) * rows_ref[pl.ds(m, 1), :]
            ratio = ratio * (1.0 / other[:, slots : slots + 1])
            jac_out[m] = jnp.where(here, eye - ratio, 0.0)[:, 0:slots]
        return carry

    lax.fori_loop(0, own // block, last_sweep, 0)

    for it in range(ITERS):
        norms_out[it] = norms[it][0, 0]
    for k in range(1, draws):
        mean_copy(k).wait()
    for d in range(draws):
        mean_out[d * own : (d + 1) * own, :] = mean_slots[d][:, 0:slots]

    for k in range(1, draws):
        for c in range(pieces):
            far_copy(k, c).wait_send()
        for g in range(1, draws + 1):
            part_copy(k, g).wait_send()
    for k in range(1, chips):
        peak_copy(k).wait_send()
    for it in range(ITERS - 1):
        peaks_all(it, peaks_send_sem).wait()


def shards(x_char, nu_draws, coef_sigma, log_share, counts):
    markets, slots, coefs = x_char.shape
    consumers = nu_draws.shape[2]
    draws, chips = lax.axis_size("draw"), lax.axis_size("mkt")
    own = markets // draws
    block = divisor_up_to(own, BLOCK)
    pieces = divisor_up_to(own, PIECES)
    vmem = pl.BlockSpec(memory_space=pltpu.VMEM)
    smem = pl.BlockSpec(memory_space=pltpu.SMEM)
    f32 = jnp.float32
    dma = pltpu.SemaphoreType.DMA
    return pl.pallas_call(
        functools.partial(kernel, draws, chips, 1.0 / (consumers * draws)),
        out_shape=(
            jax.ShapeDtypeStruct((markets, slots), f32),
            jax.ShapeDtypeStruct((own, slots, slots), f32),
            jax.ShapeDtypeStruct((ITERS,), f32),
        ),
        in_specs=[pl.BlockSpec(memory_space=pltpu.HBM)] * 6,
        out_specs=(vmem, vmem, smem),
        scratch_shapes=[
            pltpu.SMEM((coefs,), f32),
            pltpu.SMEM((markets,), jnp.int32),
            pltpu.VMEM((1, markets), jnp.int32),
            pltpu.VMEM((markets, slots), f32),
            pltpu.VMEM((markets, coefs, slots), f32),
            pltpu.VMEM((draws, own, coefs, consumers), f32),
            pltpu.VMEM((draws - 1, own, coefs, consumers), f32),
            pltpu.VMEM((own, slots, draws * consumers), f32),
            pltpu.VMEM((own, consumers), f32),
            pltpu.VMEM((block, draws * consumers // LANES, LANES), f32),
            pltpu.VMEM((own, LANES), f32),
            pltpu.VMEM((LANES, LANES), f32),
            pltpu.VMEM((LANES, LANES), f32),
            pltpu.VMEM((draws, draws, 8, LANES), f32),
            pltpu.VMEM((chips, 1, LANES), f32),
            pltpu.VMEM((ITERS - 1, chips * draws, 1, LANES), f32),
            pltpu.VMEM((draws, own, LANES), f32),
            dma((draws - 1, draws)),
            dma((draws - 1, draws)),
            dma((chips,)),
            dma((chips,)),
            dma((ITERS - 1,)),
            dma((ITERS - 1,)),
            dma((draws - 1, pieces)),
            dma((draws - 1, pieces)),
            dma((draws,)),
            dma((draws,)),
            dma((5,)),
            dma((draws,)),
        ],
        compiler_params=pltpu.CompilerParams(
            collective_id=0, has_side_effects=True, vmem_limit_bytes=VMEM_LIMIT
        ),
        name="contraction",
    )(
        *(
            pltpu.with_memory_space_constraint(operand, pltpu.HBM)
            for operand in (
                coef_sigma,
                counts,
                counts[None, :],
                log_share,
                jnp.swapaxes(x_char, 1, 2),
                nu_draws,
            )
        )
    )


def solution(mesh):
    return jax.shard_map(
        shards,
        mesh=mesh,
        in_specs=(P("mkt", None, None), P("mkt", None, "draw"), P(), P("mkt", None), P("mkt")),
        out_specs=(P("mkt", None), P(("mkt", "draw"), None, None), P()),
        check_vma=False,
    )
```

```python
import functools
import math

import jax
import jax.numpy as jnp
from jax import lax
from jax.experimental import pallas as pl
from jax.experimental.pallas import tpu as pltpu
from jax.sharding import PartitionSpec as P

ITERS = 3
LANES = 128
BLOCK = 4
PIECES = 4
EARLY = 1
VMEM_LIMIT = 48 * 1024 * 1024
MESH = pl.DeviceIdType.MESH

step_cap = 0.25
epsilon = 1e-06


def divisor_up_to(count, most):
    return max(size for size in range(1, most + 1) if count % size == 0)


def rounded(value):
    return value.astype(jnp.bfloat16).astype(jnp.float32)


def split2(value):
    first = rounded(value)
    return first, value - first


def kernel(
    draws,
    chips,
    inverse,
    sigma_hbm,
    counts_hbm,
    counts_row_hbm,
    log_share_hbm,
    x_hbm,
    nu_hbm,
    mean_out,
    jac_out,
    norms_out,
    sigma_ref,
    counts_ref,
    counts_row_ref,
    log_share_ref,
    x_ref,
    nu_ref,
    far_ref,
    held,
    first_ref,
    inverse_ref,
    rows_ref,
    square,
    turn,
    norms_ref,
    part_slots,
    peak_slots,
    peaks_slots,
    mean_slots,
    part_send_sem,
    part_recv_sem,
    peak_send_sem,
    peak_recv_sem,
    peaks_send_sem,
    peaks_recv_sem,
    far_send_sem,
    far_recv_sem,
    mean_send_sem,
    mean_recv_sem,
    load_sem,
    nu_sem,
):
    markets, coefs, slots = x_ref.shape
    own = markets // draws
    consumers = nu_ref.shape[3]
    tiles = slots // 8
    half = LANES // 2
    block = divisor_up_to(own, BLOCK)
    pieces = far_send_sem.shape[1]
    piece = own // pieces
    my_draw = lax.axis_index("draw")
    my_mkt = lax.axis_index("mkt")
    cores = 2 if draws % 2 == 0 else 1

    def partner(k):
        chip = (my_draw // cores + (k - 1) // cores + 1) % (draws // cores)
        core = (my_draw + k) % cores
        return chip * cores + core

    loads = [
        pltpu.make_async_copy(source, target, load_sem.at[n])
        for n, (source, target) in enumerate(
            (
                (counts_row_hbm, counts_row_ref),
                (log_share_hbm, log_share_ref),
                (sigma_hbm, sigma_ref),
                (counts_hbm, counts_ref),
                (x_hbm, x_ref),
            )
        )
    ]

    def nu_load(k):
        return pltpu.make_async_copy(
            nu_hbm.at[pl.ds(partner(k) * own, own)], nu_ref.at[k - 1], nu_sem.at[k - 1]
        )

    for load in loads:
        load.start()
    for k in range(1, draws + 1):
        nu_load(k).start()

    barrier = pltpu.get_barrier_semaphore()
    for k in range(1, draws):
        pl.semaphore_signal(
            barrier, inc=1, device_id={"draw": lax.rem(my_draw + k, draws)}, device_id_type=MESH
        )
    for k in range(1, chips):
        pl.semaphore_signal(
            barrier, inc=1, device_id={"mkt": lax.rem(my_mkt + k, chips)}, device_id_type=MESH
        )

    def far_copy(k, c):
        return pltpu.make_async_remote_copy(
            src_ref=nu_hbm.at[pl.ds(partner(k) * own + c * piece, piece)],
            dst_ref=far_ref.at[k - 1, pl.ds(c * piece, piece)],
            send_sem=far_send_sem.at[k - 1, c],
            recv_sem=far_recv_sem.at[k - 1, c],
            device_id={"draw": partner(k)},
            device_id_type=MESH,
        )

    near = range(max(1, draws - cores + 1), draws)
    distant = range(1, max(1, draws - cores + 1))

    lane = lax.broadcasted_iota(jnp.int32, (slots, LANES), 1)
    row = lax.broadcasted_iota(jnp.int32, (slots, LANES), 0)
    lane8 = lax.broadcasted_iota(jnp.int32, (8, LANES), 1)
    row8 = lax.broadcasted_iota(jnp.int32, (8, LANES), 0)

    square[...] = jnp.zeros_like(square)
    for load in loads:
        load.wait()
    square[0:markets, 0:slots] = log_share_ref[...]
    log_share = square[...].T[0:slots, :]
    square[0:1, 0:markets] = counts_row_ref[...].astype(jnp.float32)
    counts = square[0:1, :]
    usable = (row.astype(jnp.float32) < counts) & (lane < markets)
    inside = jnp.sum(jnp.where(usable, jnp.exp(log_share), 0.0), axis=0, keepdims=True)
    mean = jnp.where(usable, log_share - jnp.log(1.0 - inside), 0.0)
    weights = jnp.where(usable, jnp.exp(mean), 0.0)

    coef_row = lax.broadcasted_iota(jnp.int32, (coefs, slots), 0)
    sigma = jnp.zeros((coefs, slots), jnp.float32)
    for k in range(coefs):
        sigma = jnp.where(coef_row == k, sigma_ref[k] * math.log2(math.e), sigma)

    def raised_tastes(chars, draw):
        s1, s2 = split2(chars * sigma)
        n1, n2 = split2(draw)
        left = jnp.concatenate([s1, s1, s2, s2], axis=0).astype(jnp.bfloat16)
        right = jnp.concatenate([n1, n2, n1, n2], axis=0).astype(jnp.bfloat16)
        tastes = lax.dot_general(
            left, right, (((0,), (0,)), ((), ())), preferred_element_type=jnp.float32
        )
        return jnp.exp2(tastes)

    def packed(value, base):
        total = jnp.zeros((8, LANES), jnp.float32)
        for t in range(tiles):
            shift = (t * own - base) % LANES
            moved = value[8 * t : 8 * t + 8]
            moved = pltpu.roll(moved, shift, 1) if shift else moved
            total = jnp.where((lane8 >= t * own) & (lane8 < (t + 1) * own), moved, total)
        return total

    def unpacked(value):
        return jnp.concatenate(
            [pltpu.roll(value, LANES - t * own, 1) if t else value for t in range(tiles)], axis=0
        )

    def placed(part, column, i):
        for t in range(tiles):
            part = jnp.where(lane8 == t * own + i, column[8 * t : 8 * t + 8], part)
        return part

    pl.semaphore_wait(barrier, draws - 1 + chips - 1)
    for k in near:
        for c in range(pieces):
            far_copy(k, c).start()
    for c in range(min(EARLY, pieces)):
        for k in distant:
            far_copy(k, c).start()

    def part_copy(k, g):
        return pltpu.make_async_remote_copy(
            src_ref=part_slots.at[my_draw, partner(g)],
            dst_ref=part_slots.at[my_draw, partner(g)],
            send_sem=part_send_sem.at[k - 1, g - 1],
            recv_sem=part_recv_sem.at[k - 1, g - 1],
            device_id={"draw": lax.rem(my_draw + k, draws)},
            device_id_type=MESH,
        )

    mine = (draws - 1) * consumers
    near_chunks = [
        slice(at, min(at + LANES, consumers)) for at in range(0, consumers, LANES)
    ]

    def first_sweep(g, carry):
        base = partner(g) * own
        nu_load(g).wait()
        local = pltpu.roll(weights, lax.rem(LANES - base, LANES), 1)
        for i in range(own):
            weight = local[:, i : i + 1]
            known = raised_tastes(x_ref[base + i], nu_ref[g - 1, i])
            held[i, :, mine : mine + consumers] = known
            for chunk in near_chunks:
                first_ref[i : i + 1, chunk] = 1.0 + jnp.sum(
                    weight * known[:, chunk], axis=0, keepdims=True
                )
        first_ref[...] = 1.0 / first_ref[...]
        part = jnp.zeros((8, LANES), jnp.float32)
        for i in range(own):
            column = None
            for chunk in near_chunks:
                term = (
                    held[i, :, mine + chunk.start : mine + chunk.stop]
                    * first_ref[i : i + 1, chunk]
                )
                column = term if column is None else column + term
            part = placed(part, jnp.sum(column, axis=1, keepdims=True), i)
        part_slots[my_draw, partner(g)] = part
        for k in range(1, draws):
            part_copy(k, g).start()
        return carry

    lax.fori_loop(1, draws + 1, first_sweep, 0)

    for c in range(min(EARLY, pieces), pieces):
        for k in distant:
            far_copy(k, c).start()

    def fill(k, c):
        far_copy(k, c).wait_recv()

        def body(i, carry):
            m = c * piece + i
            held[m, :, (k - 1) * consumers : k * consumers] = raised_tastes(
                x_ref[my_draw * own + m], far_ref[k - 1, m]
            )
            return carry

        lax.fori_loop(0, piece, body, 0, unroll=True)

    for c in range(pieces):
        for k in near:
            fill(k, c)

    product = row8
    for t in range(1, tiles):
        product = jnp.where(lane8 >= t * own, row8 + 8 * t, product)
    wide_counts = jnp.broadcast_to(counts, (slots, LANES))
    ls, means, valid = [], [], []
    for g in range(draws):
        ls.append(packed(log_share, g * own))
        means.append(packed(mean, g * own))
        valid.append(
            (product.astype(jnp.float32) < packed(wide_counts, g * own)) & (lane8 < tiles * own)
        )

    def change_of(weight, total, ls, valid):
        shares = jnp.where(valid, weight * total * inverse, 1.0)
        return jnp.where(valid, ls - jnp.log(shares), 0.0)

    start_weights = [jnp.where(valid[g], jnp.exp(means[g]), 0.0) for g in range(draws)]
    for g in range(1, draws + 1):
        for k in range(1, draws):
            part_copy(k, g).wait_recv()
    changes = []
    peak = jnp.zeros((8, LANES), jnp.float32)
    for g in range(draws):
        total = part_slots[0, g]
        for d in range(1, draws):
            total = total + part_slots[d, g]
        changes.append(change_of(start_weights[g], total, ls[g], valid[g]))
        peak = jnp.maximum(peak, jnp.abs(changes[g]))
    peak_slots[0] = jnp.max(peak, axis=0, keepdims=True)

    def peak_copy(k):
        return pltpu.make_async_remote_copy(
            src_ref=peak_slots.at[0],
            dst_ref=peak_slots.at[k],
            send_sem=peak_send_sem.at[k - 1],
            recv_sem=peak_recv_sem.at[k - 1],
            device_id={"mkt": lax.rem(my_mkt + k, chips)},
            device_id_type=MESH,
        )

    for k in range(1, chips):
        peak_copy(k).start()

    def choose(values):
        chosen = values[0]
        for g in range(1, draws):
            chosen = jnp.where(my_draw == g, values[g], chosen)
        return chosen

    ls_own = choose(ls)
    mean_own = choose(means)
    change = choose(changes)
    count_own = choose([packed(wide_counts, g * own) for g in range(draws)])
    valid_own = (product.astype(jnp.float32) < count_own) & (lane8 < tiles * own)

    for c in range(pieces):
        for k in distant:
            fill(k, c)

    def largest_of(slots_ref):
        rows = [slots_ref[n] for n in range(slots_ref.shape[0])]
        while len(rows) > 1:
            rows = [
                jnp.maximum(rows[n], rows[n + 1]) if n + 1 < len(rows) else rows[n]
                for n in range(0, len(rows), 2)
            ]
        return jnp.max(rows[0], axis=1, keepdims=True)

    def step_of(largest):
        return jnp.minimum(1.0, step_cap / (largest + epsilon))

    for k in range(1, chips):
        peak_copy(k).wait_recv()
    norms = largest_of(peak_slots)
    mean_own = mean_own + step_of(norms) * change

    lanes_of = [slice(at, at + LANES) for at in range(0, draws * consumers, LANES)]

    def denominators(weight):
        for m in range(own):
            column = jnp.concatenate(
                [weight[:, t * own + m : t * own + m + 1] for t in range(tiles)], axis=0
            )
            for n, chunk in enumerate(lanes_of):
                inverse_ref[m, n : n + 1, :] = 1.0 + jnp.sum(
                    column * held[m, :, chunk], axis=0, keepdims=True
                )
        inverse_ref[...] = 1.0 / inverse_ref[...]

    def sweep(weight):
        denominators(weight)
        part = jnp.zeros((8, LANES), jnp.float32)
        for m in range(own):
            column = None
            for n, chunk in enumerate(lanes_of):
                term = held[m, :, chunk] * inverse_ref[m, n : n + 1, :]
                column = term if column is None else column + term
            part = placed(part, jnp.sum(column, axis=1, keepdims=True), m)
        return part

    others = [(m, d) for m in range(chips) for d in range(draws) if m or d]

    def peaks_copy(it, n):
        m, d = others[n]
        return pltpu.make_async_remote_copy(
            src_ref=peaks_slots.at[it, 0],
            dst_ref=peaks_slots.at[it, n + 1],
            send_sem=peaks_send_sem.at[it],
            recv_sem=peaks_recv_sem.at[it],
            device_id={
                "mkt": lax.rem(my_mkt + m, chips),
                "draw": lax.rem(my_draw + d, draws),
            },
            device_id_type=MESH,
        )

    def peaks_all(it, sem):
        span = peaks_slots.at[it, pl.ds(1, len(others))]
        return pltpu.make_async_copy(span, span, sem.at[it])

    norms_ref[0] = norms
    def iteration(it, mean_own):
        weight = jnp.where(valid_own, jnp.exp(mean_own), 0.0)
        change = change_of(weight, sweep(weight), ls_own, valid_own)
        peaks_slots[it, 0] = jnp.max(jnp.abs(change), axis=0, keepdims=True)
        for n in range(len(others)):
            peaks_copy(it, n).start()
        peaks_all(it, peaks_recv_sem).wait()
        largest = largest_of(peaks_slots.at[it])
        norms_ref[it + 1] = largest
        return mean_own + step_of(largest) * change

    mean_own = lax.fori_loop(0, ITERS - 1, iteration, mean_own)

    square[0:slots, :] = unpacked(mean_own)
    mean_rows = square[...].T[0:own, :]
    mean_slots[my_draw] = mean_rows
    rows_ref[...] = jnp.exp(mean_rows)

    def mean_copy(k):
        return pltpu.make_async_remote_copy(
            src_ref=mean_slots.at[my_draw],
            dst_ref=mean_slots.at[my_draw],
            send_sem=mean_send_sem.at[k - 1],
            recv_sem=mean_recv_sem.at[k - 1],
            device_id={"draw": lax.rem(my_draw + k, draws)},
            device_id_type=MESH,
        )

    for k in range(1, draws):
        mean_copy(k).start()

    weight = jnp.where(valid_own, jnp.exp(mean_own), 0.0)
    eye = jnp.where(row == lane, 1.0, 0.0)
    ones = jnp.ones((8, draws * consumers), jnp.float32)
    scale = jnp.where(lax.broadcasted_iota(jnp.int32, (half, LANES), 0) < slots, 0.5, 1.0)
    low_half = lax.broadcasted_iota(jnp.int32, (half, LANES), 1) < half

    denominators(weight)

    def last_sweep(b, carry):
        sums = []
        for u in range(block):
            chance = jnp.concatenate(
                [
                    held[b * block + u, :, chunk] * inverse_ref[b * block + u, n : n + 1, :]
                    for n, chunk in enumerate(lanes_of)
                ],
                axis=1,
            )
            low = chance - rounded(chance)
            left = jnp.concatenate([chance, ones], axis=0).astype(jnp.bfloat16)
            right = jnp.concatenate([chance, low], axis=0).astype(jnp.bfloat16)
            products = lax.dot_general(
                left, right, (((1,), (1,)), ((), ())), preferred_element_type=jnp.float32
            )
            products = jnp.concatenate(
                [products, jnp.zeros((half, LANES - 2 * slots), jnp.float32)], axis=1
            )
            sums.append(scale * products + pltpu.roll(products, LANES - slots, 1))
        for at in range(0, block, 2):
            pair = sums[at]
            if at + 1 < block:
                pair = jnp.where(low_half, pair, pltpu.roll(sums[at + 1], half, 1))
            turn[at // 2 * half : at // 2 * half + half, :] = pair
        turn[...] = turn[...].T
        for u in range(block):
            other = turn[u % 2 * half : u % 2 * half + slots, :]
            other = pltpu.roll(other, half, 1) if u // 2 else other
            m = b * block + u
            count = counts_ref[my_draw * own + m]
            here = (row < count) & (lane < count)
            ratio = (sums[u][0:slots] + other) * rows_ref[pl.ds(m, 1), :]
            ratio = ratio * (1.0 / other[:, slots : slots + 1])
            jac_out[m] = jnp.where(here, eye - ratio, 0.0)[:, 0:slots]
        return carry

    lax.fori_loop(0, own // block, last_sweep, 0, unroll=True)

    for it in range(ITERS):
        norms_out[it] = norms_ref[it][0, 0]
    for k in range(1, draws):
        mean_copy(k).wait()
    for d in range(draws):
        mean_out[d * own : (d + 1) * own, :] = mean_slots[d][:, 0:slots]

    for k in range(1, draws):
        for c in range(pieces):
            far_copy(k, c).wait_send()
        for g in range(1, draws + 1):
            part_copy(k, g).wait_send()
    for k in range(1, chips):
        peak_copy(k).wait_send()
    for it in range(ITERS - 1):
        peaks_all(it, peaks_send_sem).wait()


def store(mean, jac, norms, mean_out, jac_out, norms_out, sem):
    copies = [
        pltpu.make_async_copy(source, target, sem.at[n])
        for n, (source, target) in enumerate(
            ((jac, jac_out), (mean, mean_out), (norms, norms_out))
        )
    ]
    for copy in copies:
        copy.start()
    for copy in copies:
        copy.wait()


def shards(x_char, nu_draws, coef_sigma, log_share, counts):
    markets, slots, coefs = x_char.shape
    consumers = nu_draws.shape[2]
    draws, chips = lax.axis_size("draw"), lax.axis_size("mkt")
    own = markets // draws
    pieces = divisor_up_to(own, PIECES)
    vmem = pl.BlockSpec(memory_space=pltpu.VMEM)
    smem = pl.BlockSpec(memory_space=pltpu.SMEM)
    f32 = jnp.float32
    dma = pltpu.SemaphoreType.DMA
    results = pl.pallas_call(
        functools.partial(kernel, draws, chips, 1.0 / (consumers * draws)),
        out_shape=(
            jax.ShapeDtypeStruct((markets, slots), f32),
            jax.ShapeDtypeStruct((own, slots, slots), f32),
            jax.ShapeDtypeStruct((ITERS,), f32),
        ),
        in_specs=[pl.BlockSpec(memory_space=pltpu.HBM)] * 6,
        out_specs=(vmem, vmem, smem),
        scratch_shapes=[
            pltpu.SMEM((coefs,), f32),
            pltpu.SMEM((markets,), jnp.int32),
            pltpu.VMEM((1, markets), jnp.int32),
            pltpu.VMEM((markets, slots), f32),
            pltpu.VMEM((markets, coefs, slots), f32),
            pltpu.VMEM((draws, own, coefs, consumers), f32),
            pltpu.VMEM((draws - 1, own, coefs, consumers), f32),
            pltpu.VMEM((own, slots, draws * consumers), f32),
            pltpu.VMEM((own, consumers), f32),
            pltpu.VMEM((own, draws * consumers // LANES, LANES), f32),
            pltpu.VMEM((own, LANES), f32),
            pltpu.VMEM((LANES, LANES), f32),
            pltpu.VMEM((LANES, LANES), f32),
            pltpu.VMEM((ITERS, 1, 1), f32),
            pltpu.VMEM((draws, draws, 8, LANES), f32),
            pltpu.VMEM((chips, 1, LANES), f32),
            pltpu.VMEM((ITERS - 1, chips * draws, 1, LANES), f32),
            pltpu.VMEM((draws, own, LANES), f32),
            dma((draws - 1, draws)),
            dma((draws - 1, draws)),
            dma((chips,)),
            dma((chips,)),
            dma((ITERS - 1,)),
            dma((ITERS - 1,)),
            dma((draws - 1, pieces)),
            dma((draws - 1, pieces)),
            dma((draws,)),
            dma((draws,)),
            dma((5,)),
            dma((draws,)),
        ],
        compiler_params=pltpu.CompilerParams(
            collective_id=0, has_side_effects=True, vmem_limit_bytes=VMEM_LIMIT
        ),
        name="contraction",
    )(
        *(
            pltpu.with_memory_space_constraint(operand, pltpu.HBM)
            for operand in (
                coef_sigma,
                counts,
                counts[None, :],
                log_share,
                jnp.swapaxes(x_char, 1, 2),
                nu_draws,
            )
        )
    )
    hbm = pl.BlockSpec(memory_space=pltpu.HBM)
    return pl.pallas_call(
        store,
        out_shape=tuple(jax.ShapeDtypeStruct(r.shape, r.dtype) for r in results),
        in_specs=[vmem, vmem, vmem],
        out_specs=(hbm, hbm, hbm),
        scratch_shapes=[dma((3,))],
        name="store",
    )(*(pltpu.with_memory_space_constraint(r, pltpu.VMEM) for r in results))


def solution(mesh):
    return jax.shard_map(
        shards,
        mesh=mesh,
        in_specs=(P("mkt", None, None), P("mkt", None, "draw"), P(), P("mkt", None), P("mkt")),
        out_specs=(P("mkt", None), P(("mkt", "draw"), None, None), P()),
        check_vma=False,
    )
```

```python
import functools
import math

import jax
import jax.numpy as jnp
from jax import lax
from jax.experimental import pallas as pl
from jax.experimental.pallas import tpu as pltpu
from jax.sharding import PartitionSpec as P

ITERS = 3
LANES = 128
BLOCK = 4
PIECES = 4
EARLY = 1
VMEM_LIMIT = 48 * 1024 * 1024
MESH = pl.DeviceIdType.MESH

step_cap = 0.25
epsilon = 1e-06


def divisor_up_to(count, most):
    return max(size for size in range(1, most + 1) if count % size == 0)


def rounded(value):
    return value.astype(jnp.bfloat16).astype(jnp.float32)


def split2(value):
    first = rounded(value)
    return first, value - first


def kernel(
    draws,
    chips,
    inverse,
    sigma_hbm,
    counts_hbm,
    counts_row_hbm,
    log_share_hbm,
    x_hbm,
    nu_hbm,
    mean_out,
    jac_out,
    norms_out,
    sigma_ref,
    counts_ref,
    counts_row_ref,
    log_share_ref,
    x_ref,
    nu_ref,
    far_ref,
    held,
    first_ref,
    inverse_ref,
    rows_ref,
    square,
    turn,
    norms_ref,
    part_slots,
    peak_slots,
    peaks_slots,
    mean_slots,
    part_send_sem,
    part_recv_sem,
    peak_send_sem,
    peak_recv_sem,
    peaks_send_sem,
    peaks_recv_sem,
    far_send_sem,
    far_recv_sem,
    mean_send_sem,
    mean_recv_sem,
    relay_sem,
    load_sem,
    nu_sem,
):
    markets, coefs, slots = x_ref.shape
    own = markets // draws
    consumers = nu_ref.shape[3]
    tiles = slots // 8
    half = LANES // 2
    block = divisor_up_to(own, BLOCK)
    pieces = far_send_sem.shape[1]
    piece = own // pieces
    my_draw = lax.axis_index("draw")
    my_mkt = lax.axis_index("mkt")
    cores = 2 if draws % 2 == 0 else 1

    def partner(k):
        chip = (my_draw // cores + (k - 1) // cores + 1) % (draws // cores)
        core = (my_draw + k) % cores
        return chip * cores + core

    loads = [
        pltpu.make_async_copy(source, target, load_sem.at[n])
        for n, (source, target) in enumerate(
            (
                (counts_row_hbm, counts_row_ref),
                (log_share_hbm, log_share_ref),
                (sigma_hbm, sigma_ref),
                (counts_hbm, counts_ref),
                (x_hbm, x_ref),
            )
        )
    ]

    def nu_load(k):
        return pltpu.make_async_copy(
            nu_hbm.at[pl.ds(partner(k) * own, own)], nu_ref.at[k - 1], nu_sem.at[k - 1]
        )

    for load in loads:
        load.start()
    for k in range(1, draws + 1):
        nu_load(k).start()

    barrier = pltpu.get_barrier_semaphore()
    for k in range(1, draws):
        pl.semaphore_signal(
            barrier, inc=1, device_id={"draw": lax.rem(my_draw + k, draws)}, device_id_type=MESH
        )

    def beside(k):
        return (my_mkt + k >= 0) & (my_mkt + k < chips)

    def signal_mkt(sem, spans):
        for k in spans:

            @pl.when(beside(k))
            def _(k=k):
                pl.semaphore_signal(
                    sem, inc=1, device_id={"mkt": my_mkt + k}, device_id_type=MESH
                )

    def wait_mkt(sem, spans, more=0):
        count = more
        for k in spans:
            count = count + jnp.where(beside(k), 1, 0)
        pl.semaphore_wait(sem, count)

    spans = [k for k in (-2, -1, 1, 2) if abs(k) < chips]
    signal_mkt(barrier, spans)

    def far_copy(k, c):
        return pltpu.make_async_remote_copy(
            src_ref=nu_hbm.at[pl.ds(partner(k) * own + c * piece, piece)],
            dst_ref=far_ref.at[k - 1, pl.ds(c * piece, piece)],
            send_sem=far_send_sem.at[k - 1, c],
            recv_sem=far_recv_sem.at[k - 1, c],
            device_id={"draw": partner(k)},
            device_id_type=MESH,
        )

    near = range(max(1, draws - cores + 1), draws)
    distant = range(1, max(1, draws - cores + 1))

    lane = lax.broadcasted_iota(jnp.int32, (slots, LANES), 1)
    row = lax.broadcasted_iota(jnp.int32, (slots, LANES), 0)
    lane8 = lax.broadcasted_iota(jnp.int32, (8, LANES), 1)
    row8 = lax.broadcasted_iota(jnp.int32, (8, LANES), 0)

    wait_mkt(barrier, spans, draws - 1)
    for k in near:
        for c in range(pieces):
            far_copy(k, c).start()
    for c in range(min(EARLY, pieces)):
        for k in distant:
            far_copy(k, c).start()
    hops = relay_sem.shape[0]
    signal_mkt(relay_sem.at[0], (-2, 2))

    square[...] = jnp.zeros_like(square)
    for load in loads:
        load.wait()
    square[0:markets, 0:slots] = log_share_ref[...]
    log_share = square[...].T[0:slots, :]
    square[0:1, 0:markets] = counts_row_ref[...].astype(jnp.float32)
    counts = square[0:1, :]
    usable = (row.astype(jnp.float32) < counts) & (lane < markets)
    inside = jnp.sum(jnp.where(usable, jnp.exp(log_share), 0.0), axis=0, keepdims=True)
    mean = jnp.where(usable, log_share - jnp.log(1.0 - inside), 0.0)
    weights = jnp.where(usable, jnp.exp(mean), 0.0)

    coef_row = lax.broadcasted_iota(jnp.int32, (coefs, slots), 0)
    sigma = jnp.zeros((coefs, slots), jnp.float32)
    for k in range(coefs):
        sigma = jnp.where(coef_row == k, sigma_ref[k] * math.log2(math.e), sigma)

    def raised_tastes(chars, draw):
        s1, s2 = split2(chars * sigma)
        n1, n2 = split2(draw)
        left = jnp.concatenate([s1, s1, s2, s2], axis=0).astype(jnp.bfloat16)
        right = jnp.concatenate([n1, n2, n1, n2], axis=0).astype(jnp.bfloat16)
        tastes = lax.dot_general(
            left, right, (((0,), (0,)), ((), ())), preferred_element_type=jnp.float32
        )
        return jnp.exp2(tastes)

    def packed(value, base):
        total = jnp.zeros((8, LANES), jnp.float32)
        for t in range(tiles):
            shift = (t * own - base) % LANES
            moved = value[8 * t : 8 * t + 8]
            moved = pltpu.roll(moved, shift, 1) if shift else moved
            total = jnp.where((lane8 >= t * own) & (lane8 < (t + 1) * own), moved, total)
        return total

    def placed(part, column, i):
        for t in range(tiles):
            part = jnp.where(lane8 == t * own + i, column[8 * t : 8 * t + 8], part)
        return part

    def part_copy(k, g):
        return pltpu.make_async_remote_copy(
            src_ref=part_slots.at[my_draw, partner(g)],
            dst_ref=part_slots.at[my_draw, partner(g)],
            send_sem=part_send_sem.at[k - 1, g - 1],
            recv_sem=part_recv_sem.at[k - 1, g - 1],
            device_id={"draw": lax.rem(my_draw + k, draws)},
            device_id_type=MESH,
        )

    mine = (draws - 1) * consumers
    near_chunks = [
        slice(at, min(at + LANES, consumers)) for at in range(0, consumers, LANES)
    ]

    def first_sweep(g, carry):
        base = partner(g) * own
        nu_load(g).wait()
        local = pltpu.roll(weights, lax.rem(LANES - base, LANES), 1)
        for i in range(own):
            weight = local[:, i : i + 1]
            known = raised_tastes(x_ref[base + i], nu_ref[g - 1, i])
            held[i, :, mine : mine + consumers] = known
            for chunk in near_chunks:
                first_ref[i : i + 1, chunk] = 1.0 + jnp.sum(
                    weight * known[:, chunk], axis=0, keepdims=True
                )
        first_ref[...] = 1.0 / first_ref[...]
        part = jnp.zeros((8, LANES), jnp.float32)
        for i in range(own):
            column = None
            for chunk in near_chunks:
                term = (
                    held[i, :, mine + chunk.start : mine + chunk.stop]
                    * first_ref[i : i + 1, chunk]
                )
                column = term if column is None else column + term
            part = placed(part, jnp.sum(column, axis=1, keepdims=True), i)
        part_slots[my_draw, partner(g)] = part
        for k in range(1, draws):
            part_copy(k, g).start()
        return carry

    lax.fori_loop(1, draws + 1, first_sweep, 0)

    for c in range(min(EARLY, pieces), pieces):
        for k in distant:
            far_copy(k, c).start()
    for hop in range(hops - 1):
        reach = 2 << hop
        wait_mkt(relay_sem.at[hop], (-reach, reach))
        signal_mkt(relay_sem.at[hop + 1], (-2 * reach, 2 * reach))

    def fill(k, c):
        far_copy(k, c).wait_recv()

        def body(i, carry):
            m = c * piece + i
            held[m, :, (k - 1) * consumers : k * consumers] = raised_tastes(
                x_ref[my_draw * own + m], far_ref[k - 1, m]
            )
            return carry

        lax.fori_loop(0, piece, body, 0, unroll=True)

    for c in range(pieces):
        for k in near:
            fill(k, c)

    product = row8
    for t in range(1, tiles):
        product = jnp.where(lane8 >= t * own, row8 + 8 * t, product)
    wide_counts = jnp.broadcast_to(counts, (slots, LANES))
    ls, means, valid = [], [], []
    for g in range(draws):
        ls.append(packed(log_share, g * own))
        means.append(packed(mean, g * own))
        valid.append(
            (product.astype(jnp.float32) < packed(wide_counts, g * own)) & (lane8 < tiles * own)
        )

    def change_of(weight, total, ls, valid):
        shares = jnp.where(valid, weight * total * inverse, 1.0)
        return jnp.where(valid, ls - jnp.log(shares), 0.0)

    start_weights = [jnp.where(valid[g], jnp.exp(means[g]), 0.0) for g in range(draws)]
    for g in range(1, draws + 1):
        for k in range(1, draws):
            part_copy(k, g).wait_recv()
    changes = []
    peak = jnp.zeros((8, LANES), jnp.float32)
    for g in range(draws):
        total = part_slots[0, g]
        for d in range(1, draws):
            total = total + part_slots[d, g]
        changes.append(change_of(start_weights[g], total, ls[g], valid[g]))
        peak = jnp.maximum(peak, jnp.abs(changes[g]))
    peak_slots[0] = jnp.max(peak, axis=0, keepdims=True)

    def peak_copy(k):
        return pltpu.make_async_remote_copy(
            src_ref=peak_slots.at[0],
            dst_ref=peak_slots.at[k],
            send_sem=peak_send_sem.at[k - 1],
            recv_sem=peak_recv_sem.at[k - 1],
            device_id={"mkt": lax.rem(my_mkt + k, chips)},
            device_id_type=MESH,
        )

    wait_mkt(relay_sem.at[hops - 1], (-(2 << hops - 1), 2 << hops - 1))
    for k in range(1, chips):
        peak_copy(k).start()

    def choose(values):
        chosen = values[0]
        for g in range(1, draws):
            chosen = jnp.where(my_draw == g, values[g], chosen)
        return chosen

    ls_own = choose(ls)
    mean_own = choose(means)
    change = choose(changes)
    count_own = choose([packed(wide_counts, g * own) for g in range(draws)])
    valid_own = (product.astype(jnp.float32) < count_own) & (lane8 < tiles * own)

    for c in range(pieces):
        for k in distant:
            fill(k, c)

    def largest_of(slots_ref):
        rows = [slots_ref[n] for n in range(slots_ref.shape[0])]
        while len(rows) > 1:
            rows = [
                jnp.maximum(rows[n], rows[n + 1]) if n + 1 < len(rows) else rows[n]
                for n in range(0, len(rows), 2)
            ]
        return jnp.max(rows[0], axis=1, keepdims=True)

    def step_of(largest):
        return jnp.minimum(1.0, step_cap / (largest + epsilon))

    for k in range(1, chips):
        peak_copy(k).wait_recv()
    norms = largest_of(peak_slots)
    mean_own = mean_own + step_of(norms) * change

    lanes_of = [slice(at, at + LANES) for at in range(0, draws * consumers, LANES)]

    def denominators(weight):
        for m in range(own):
            column = jnp.concatenate(
                [weight[:, t * own + m : t * own + m + 1] for t in range(tiles)], axis=0
            )
            for n, chunk in enumerate(lanes_of):
                inverse_ref[m, n : n + 1, :] = 1.0 + jnp.sum(
                    column * held[m, :, chunk], axis=0, keepdims=True
                )
        inverse_ref[...] = 1.0 / inverse_ref[...]

    def sweep(weight):
        denominators(weight)
        part = jnp.zeros((8, LANES), jnp.float32)
        for m in range(own):
            column = None
            for n, chunk in enumerate(lanes_of):
                term = held[m, :, chunk] * inverse_ref[m, n : n + 1, :]
                column = term if column is None else column + term
            part = placed(part, jnp.sum(column, axis=1, keepdims=True), m)
        return part

    others = [(m, d) for m in range(chips) for d in range(draws) if m or d]

    def peaks_copy(it, n):
        m, d = others[n]
        return pltpu.make_async_remote_copy(
            src_ref=peaks_slots.at[it, 0],
            dst_ref=peaks_slots.at[it, n + 1],
            send_sem=peaks_send_sem.at[it],
            recv_sem=peaks_recv_sem.at[it],
            device_id={
                "mkt": lax.rem(my_mkt + m, chips),
                "draw": lax.rem(my_draw + d, draws),
            },
            device_id_type=MESH,
        )

    def peaks_all(it, sem):
        span = peaks_slots.at[it, pl.ds(1, len(others))]
        return pltpu.make_async_copy(span, span, sem.at[it])

    def mean_copy(k):
        return pltpu.make_async_remote_copy(
            src_ref=mean_slots.at[my_draw],
            dst_ref=mean_slots.at[my_draw],
            send_sem=mean_send_sem.at[k - 1],
            recv_sem=mean_recv_sem.at[k - 1],
            device_id={"draw": lax.rem(my_draw + k, draws)},
            device_id_type=MESH,
        )

    norms_ref[0] = norms
    def iteration(it, mean_own):
        weight = jnp.where(valid_own, jnp.exp(mean_own), 0.0)
        change = change_of(weight, sweep(weight), ls_own, valid_own)
        peaks_slots[it, 0] = jnp.max(jnp.abs(change), axis=0, keepdims=True)
        for n in range(len(others)):
            peaks_copy(it, n).start()

        @pl.when(it == ITERS - 2)
        def _():
            mean_slots[my_draw, 0] = mean_own
            mean_slots[my_draw, 1] = change
            for k in range(1, draws):
                mean_copy(k).start()

        peaks_all(it, peaks_recv_sem).wait()
        largest = largest_of(peaks_slots.at[it])
        norms_ref[it + 1] = largest
        return mean_own + step_of(largest) * change

    mean_own = lax.fori_loop(0, ITERS - 1, iteration, mean_own)

    for k in range(1, draws):
        mean_copy(k).wait_recv()
    step = step_of(norms_ref[ITERS - 1])
    mean_tiles = [mean_slots[d, 0] + step * mean_slots[d, 1] for d in range(draws)]
    for t in range(tiles):
        total = mean_tiles[0]
        total = pltpu.roll(total, LANES - t * own, 1) if t else total
        for d in range(1, draws):
            shift = (d - t) * own % LANES
            moved = pltpu.roll(mean_tiles[d], shift, 1) if shift else mean_tiles[d]
            total = jnp.where(lane8 >= d * own, moved, total)
        square[8 * t : 8 * t + 8, :] = total
    mean_rows = square[...].T
    mean_out[...] = mean_rows[0:markets, 0:slots]
    rows_ref[...] = jnp.exp(mean_rows[0:markets])

    weight = jnp.where(valid_own, jnp.exp(mean_own), 0.0)
    eye = jnp.where(row == lane, 1.0, 0.0)
    ones = jnp.ones((8, draws * consumers), jnp.float32)
    scale = jnp.where(lax.broadcasted_iota(jnp.int32, (half, LANES), 0) < slots, 0.5, 1.0)
    low_half = lax.broadcasted_iota(jnp.int32, (half, LANES), 1) < half

    denominators(weight)

    def last_sweep(b, carry):
        sums = []
        for u in range(block):
            chance = jnp.concatenate(
                [
                    held[b * block + u, :, chunk] * inverse_ref[b * block + u, n : n + 1, :]
                    for n, chunk in enumerate(lanes_of)
                ],
                axis=1,
            )
            low = chance - rounded(chance)
            left = jnp.concatenate([chance, ones], axis=0).astype(jnp.bfloat16)
            right = jnp.concatenate([chance, low], axis=0).astype(jnp.bfloat16)
            products = lax.dot_general(
                left, right, (((1,), (1,)), ((), ())), preferred_element_type=jnp.float32
            )
            products = jnp.concatenate(
                [products, jnp.zeros((half, LANES - 2 * slots), jnp.float32)], axis=1
            )
            sums.append(scale * products + pltpu.roll(products, LANES - slots, 1))
        for at in range(0, block, 2):
            pair = sums[at]
            if at + 1 < block:
                pair = jnp.where(low_half, pair, pltpu.roll(sums[at + 1], half, 1))
            turn[at // 2 * half : at // 2 * half + half, :] = pair
        turn[...] = turn[...].T
        for u in range(block):
            other = turn[u % 2 * half : u % 2 * half + slots, :]
            other = pltpu.roll(other, half, 1) if u // 2 else other
            m = b * block + u
            count = counts_ref[my_draw * own + m]
            here = (row < count) & (lane < count)
            ratio = (sums[u][0:slots] + other) * rows_ref[pl.ds(my_draw * own + m, 1), :]
            ratio = ratio * (1.0 / other[:, slots : slots + 1])
            jac_out[m] = jnp.where(here, eye - ratio, 0.0)[:, 0:slots]
        return carry

    lax.fori_loop(0, own // block, last_sweep, 0, unroll=True)

    for it in range(ITERS):
        norms_out[it] = norms_ref[it][0, 0]
    for k in range(1, draws):
        mean_copy(k).wait_send()
        for c in range(pieces):
            far_copy(k, c).wait_send()
        for g in range(1, draws + 1):
            part_copy(k, g).wait_send()
    for k in range(1, chips):
        peak_copy(k).wait_send()
    for it in range(ITERS - 1):
        peaks_all(it, peaks_send_sem).wait()


def store(mean, jac, norms, mean_out, jac_out, norms_out, sem):
    copies = [
        pltpu.make_async_copy(source, target, sem.at[n])
        for n, (source, target) in enumerate(
            ((jac, jac_out), (mean, mean_out), (norms, norms_out))
        )
    ]
    for copy in copies:
        copy.start()
    for copy in copies:
        copy.wait()


def shards(x_char, nu_draws, coef_sigma, log_share, counts):
    markets, slots, coefs = x_char.shape
    consumers = nu_draws.shape[2]
    draws, chips = lax.axis_size("draw"), lax.axis_size("mkt")
    own = markets // draws
    pieces = divisor_up_to(own, PIECES)
    vmem = pl.BlockSpec(memory_space=pltpu.VMEM)
    smem = pl.BlockSpec(memory_space=pltpu.SMEM)
    f32 = jnp.float32
    dma = pltpu.SemaphoreType.DMA
    results = pl.pallas_call(
        functools.partial(kernel, draws, chips, 1.0 / (consumers * draws)),
        out_shape=(
            jax.ShapeDtypeStruct((markets, slots), f32),
            jax.ShapeDtypeStruct((own, slots, slots), f32),
            jax.ShapeDtypeStruct((ITERS,), f32),
        ),
        in_specs=[pl.BlockSpec(memory_space=pltpu.HBM)] * 6,
        out_specs=(vmem, vmem, smem),
        scratch_shapes=[
            pltpu.SMEM((coefs,), f32),
            pltpu.SMEM((markets,), jnp.int32),
            pltpu.VMEM((1, markets), jnp.int32),
            pltpu.VMEM((markets, slots), f32),
            pltpu.VMEM((markets, coefs, slots), f32),
            pltpu.VMEM((draws, own, coefs, consumers), f32),
            pltpu.VMEM((draws - 1, own, coefs, consumers), f32),
            pltpu.VMEM((own, slots, draws * consumers), f32),
            pltpu.VMEM((own, consumers), f32),
            pltpu.VMEM((own, draws * consumers // LANES, LANES), f32),
            pltpu.VMEM((markets, LANES), f32),
            pltpu.VMEM((LANES, LANES), f32),
            pltpu.VMEM((LANES, LANES), f32),
            pltpu.VMEM((ITERS, 1, 1), f32),
            pltpu.VMEM((draws, draws, 8, LANES), f32),
            pltpu.VMEM((chips, 1, LANES), f32),
            pltpu.VMEM((ITERS - 1, chips * draws, 1, LANES), f32),
            pltpu.VMEM((draws, 2, 8, LANES), f32),
            dma((draws - 1, draws)),
            dma((draws - 1, draws)),
            dma((chips,)),
            dma((chips,)),
            dma((ITERS - 1,)),
            dma((ITERS - 1,)),
            dma((draws - 1, pieces)),
            dma((draws - 1, pieces)),
            dma((draws,)),
            dma((draws,)),
            pltpu.SemaphoreType.REGULAR((max(1, (chips - 1).bit_length() - 1),)),
            dma((5,)),
            dma((draws,)),
        ],
        compiler_params=pltpu.CompilerParams(
            collective_id=0, has_side_effects=True, vmem_limit_bytes=VMEM_LIMIT
        ),
        name="contraction",
    )(
        *(
            pltpu.with_memory_space_constraint(operand, pltpu.HBM)
            for operand in (
                coef_sigma,
                counts,
                counts[None, :],
                log_share,
                jnp.swapaxes(x_char, 1, 2),
                nu_draws,
            )
        )
    )
    hbm = pl.BlockSpec(memory_space=pltpu.HBM)
    return pl.pallas_call(
        store,
        out_shape=tuple(jax.ShapeDtypeStruct(r.shape, r.dtype) for r in results),
        in_specs=[vmem, vmem, vmem],
        out_specs=(hbm, hbm, hbm),
        scratch_shapes=[dma((3,))],
        name="store",
    )(*(pltpu.with_memory_space_constraint(r, pltpu.VMEM) for r in results))


def solution(mesh):
    return jax.shard_map(
        shards,
        mesh=mesh,
        in_specs=(P("mkt", None, None), P("mkt", None, "draw"), P(), P("mkt", None), P("mkt")),
        out_specs=(P("mkt", None), P(("mkt", "draw"), None, None), P()),
        check_vma=False,
    )
```

```python
import functools
import math

import jax
import jax.numpy as jnp
from jax import lax
from jax.experimental import pallas as pl
from jax.experimental.pallas import tpu as pltpu
from jax.sharding import PartitionSpec as P

ITERS = 3
LANES = 128
BLOCK = 4
PIECES = 4
EARLY = 1
VMEM_LIMIT = 48 * 1024 * 1024
MESH = pl.DeviceIdType.MESH

step_cap = 0.25
epsilon = 1e-06


def divisor_up_to(count, most):
    return max(size for size in range(1, most + 1) if count % size == 0)


def rounded(value):
    return value.astype(jnp.bfloat16).astype(jnp.float32)


def split2(value):
    first = rounded(value)
    return first, value - first


def kernel(
    draws,
    chips,
    inverse,
    sigma_hbm,
    counts_hbm,
    counts_row_hbm,
    log_share_hbm,
    x_hbm,
    nu_hbm,
    mean_out,
    jac_out,
    norms_out,
    sigma_ref,
    counts_ref,
    counts_row_ref,
    log_share_ref,
    x_ref,
    nu_ref,
    far_ref,
    held,
    first_ref,
    inverse_ref,
    rows_ref,
    square,
    turn,
    norms_ref,
    part_slots,
    peak_slots,
    peaks_slots,
    mean_slots,
    part_send_sem,
    part_recv_sem,
    peak_send_sem,
    peak_recv_sem,
    peaks_send_sem,
    peaks_recv_sem,
    far_send_sem,
    far_recv_sem,
    mean_send_sem,
    mean_recv_sem,
    relay_sem,
    load_sem,
    nu_sem,
):
    markets, coefs, slots = x_ref.shape
    own = markets // draws
    consumers = nu_ref.shape[3]
    tiles = slots // 8
    half = LANES // 2
    block = divisor_up_to(own, BLOCK)
    pieces = far_send_sem.shape[1]
    piece = own // pieces
    my_draw = lax.axis_index("draw")
    my_mkt = lax.axis_index("mkt")
    cores = 2 if draws % 2 == 0 else 1

    def partner(k):
        chip = (my_draw // cores + (k - 1) // cores + 1) % (draws // cores)
        core = (my_draw + k) % cores
        return chip * cores + core

    loads = [
        pltpu.make_async_copy(source, target, load_sem.at[n])
        for n, (source, target) in enumerate(
            (
                (counts_row_hbm, counts_row_ref),
                (log_share_hbm, log_share_ref),
                (sigma_hbm, sigma_ref),
                (counts_hbm, counts_ref),
                (x_hbm, x_ref),
            )
        )
    ]

    def nu_load(k):
        return pltpu.make_async_copy(
            nu_hbm.at[pl.ds(partner(k) * own, own)], nu_ref.at[k - 1], nu_sem.at[k - 1]
        )

    for load in loads:
        load.start()
    for k in range(1, draws + 1):
        nu_load(k).start()

    barrier = pltpu.get_barrier_semaphore()
    for k in range(1, draws):
        pl.semaphore_signal(
            barrier, inc=1, device_id={"draw": lax.rem(my_draw + k, draws)}, device_id_type=MESH
        )

    def beside(k):
        return (my_mkt + k >= 0) & (my_mkt + k < chips)

    def signal_mkt(sem, spans):
        for k in spans:

            @pl.when(beside(k))
            def _(k=k):
                pl.semaphore_signal(
                    sem, inc=1, device_id={"mkt": my_mkt + k}, device_id_type=MESH
                )

    def wait_mkt(sem, spans, more=0):
        count = more
        for k in spans:
            count = count + jnp.where(beside(k), 1, 0)
        pl.semaphore_wait(sem, count)

    spans = [k for k in (-2, -1, 1, 2) if abs(k) < chips]
    signal_mkt(barrier, spans)

    def far_copy(k, c):
        return pltpu.make_async_remote_copy(
            src_ref=nu_hbm.at[pl.ds(partner(k) * own + c * piece, piece)],
            dst_ref=far_ref.at[k - 1, pl.ds(c * piece, piece)],
            send_sem=far_send_sem.at[k - 1, c],
            recv_sem=far_recv_sem.at[k - 1, c],
            device_id={"draw": partner(k)},
            device_id_type=MESH,
        )

    near = range(max(1, draws - cores + 1), draws)
    distant = range(1, max(1, draws - cores + 1))

    lane = lax.broadcasted_iota(jnp.int32, (slots, LANES), 1)
    row = lax.broadcasted_iota(jnp.int32, (slots, LANES), 0)
    lane8 = lax.broadcasted_iota(jnp.int32, (8, LANES), 1)
    row8 = lax.broadcasted_iota(jnp.int32, (8, LANES), 0)

    wait_mkt(barrier, spans, draws - 1)
    for c in range(min(EARLY, pieces)):
        for k in distant:
            far_copy(k, c).start()
    for k in near:
        for c in range(pieces):
            far_copy(k, c).start()
    hops = relay_sem.shape[0]
    signal_mkt(relay_sem.at[0], (-2, 2))

    square[...] = jnp.zeros_like(square)
    for load in loads:
        load.wait()
    square[0:markets, 0:slots] = log_share_ref[...]
    log_share = square[...].T[0:slots, :]
    square[0:1, 0:markets] = counts_row_ref[...].astype(jnp.float32)
    counts = square[0:1, :]
    usable = (row.astype(jnp.float32) < counts) & (lane < markets)
    inside = jnp.sum(jnp.where(usable, jnp.exp(log_share), 0.0), axis=0, keepdims=True)
    mean = jnp.where(usable, log_share - jnp.log(1.0 - inside), 0.0)
    weights = jnp.where(usable, jnp.exp(mean), 0.0)

    coef_row = lax.broadcasted_iota(jnp.int32, (coefs, slots), 0)
    sigma = jnp.zeros((coefs, slots), jnp.float32)
    for k in range(coefs):
        sigma = jnp.where(coef_row == k, sigma_ref[k] * math.log2(math.e), sigma)

    def raised_tastes(chars, draw):
        s1, s2 = split2(chars * sigma)
        n1, n2 = split2(draw)
        left = jnp.concatenate([s1, s1, s2, s2], axis=0).astype(jnp.bfloat16)
        right = jnp.concatenate([n1, n2, n1, n2], axis=0).astype(jnp.bfloat16)
        tastes = lax.dot_general(
            left, right, (((0,), (0,)), ((), ())), preferred_element_type=jnp.float32
        )
        return jnp.exp2(tastes)

    def packed(value, base):
        total = jnp.zeros((8, LANES), jnp.float32)
        for t in range(tiles):
            shift = (t * own - base) % LANES
            moved = value[8 * t : 8 * t + 8]
            moved = pltpu.roll(moved, shift, 1) if shift else moved
            total = jnp.where((lane8 >= t * own) & (lane8 < (t + 1) * own), moved, total)
        return total

    def placed(part, column, i):
        for t in range(tiles):
            part = jnp.where(lane8 == t * own + i, column[8 * t : 8 * t + 8], part)
        return part

    def part_copy(k, g):
        return pltpu.make_async_remote_copy(
            src_ref=part_slots.at[my_draw, partner(g)],
            dst_ref=part_slots.at[my_draw, partner(g)],
            send_sem=part_send_sem.at[k - 1, g - 1],
            recv_sem=part_recv_sem.at[k - 1, g - 1],
            device_id={"draw": lax.rem(my_draw + k, draws)},
            device_id_type=MESH,
        )

    mine = (draws - 1) * consumers
    near_chunks = [
        slice(at, min(at + LANES, consumers)) for at in range(0, consumers, LANES)
    ]

    def first_sweep(g, carry):
        base = partner(g) * own
        nu_load(g).wait()
        local = pltpu.roll(weights, lax.rem(LANES - base, LANES), 1)
        for i in range(own):
            weight = local[:, i : i + 1]
            known = raised_tastes(x_ref[base + i], nu_ref[g - 1, i])
            held[i, :, mine : mine + consumers] = known
            for chunk in near_chunks:
                first_ref[i : i + 1, chunk] = 1.0 + jnp.sum(
                    weight * known[:, chunk], axis=0, keepdims=True
                )
        first_ref[...] = 1.0 / first_ref[...]
        part = jnp.zeros((8, LANES), jnp.float32)
        for i in range(own):
            column = None
            for chunk in near_chunks:
                term = (
                    held[i, :, mine + chunk.start : mine + chunk.stop]
                    * first_ref[i : i + 1, chunk]
                )
                column = term if column is None else column + term
            part = placed(part, jnp.sum(column, axis=1, keepdims=True), i)
        part_slots[my_draw, partner(g)] = part
        for k in range(1, draws):
            part_copy(k, g).start()
        return carry

    lax.fori_loop(1, draws + 1, first_sweep, 0)

    for c in range(min(EARLY, pieces), pieces):
        for k in distant:
            far_copy(k, c).start()
    for hop in range(hops - 1):
        reach = 2 << hop
        wait_mkt(relay_sem.at[hop], (-reach, reach))
        signal_mkt(relay_sem.at[hop + 1], (-2 * reach, 2 * reach))

    def fill(k, c):
        far_copy(k, c).wait_recv()

        def body(i, carry):
            m = c * piece + i
            held[m, :, (k - 1) * consumers : k * consumers] = raised_tastes(
                x_ref[my_draw * own + m], far_ref[k - 1, m]
            )
            return carry

        lax.fori_loop(0, piece, body, 0, unroll=True)

    for c in range(pieces):
        for k in near:
            fill(k, c)

    product = row8
    for t in range(1, tiles):
        product = jnp.where(lane8 >= t * own, row8 + 8 * t, product)
    wide_counts = jnp.broadcast_to(counts, (slots, LANES))
    ls, means, valid = [], [], []
    for g in range(draws):
        ls.append(packed(log_share, g * own))
        means.append(packed(mean, g * own))
        valid.append(
            (product.astype(jnp.float32) < packed(wide_counts, g * own)) & (lane8 < tiles * own)
        )

    def change_of(weight, total, ls, valid):
        shares = jnp.where(valid, weight * total * inverse, 1.0)
        return jnp.where(valid, ls - jnp.log(shares), 0.0)

    start_weights = [jnp.where(valid[g], jnp.exp(means[g]), 0.0) for g in range(draws)]
    for g in range(1, draws + 1):
        for k in range(1, draws):
            part_copy(k, g).wait_recv()
    changes = []
    peak = jnp.zeros((8, LANES), jnp.float32)
    for g in range(draws):
        total = part_slots[0, g]
        for d in range(1, draws):
            total = total + part_slots[d, g]
        changes.append(change_of(start_weights[g], total, ls[g], valid[g]))
        peak = jnp.maximum(peak, jnp.abs(changes[g]))
    peak_slots[0] = jnp.max(peak, axis=0, keepdims=True)

    def peak_copy(k):
        return pltpu.make_async_remote_copy(
            src_ref=peak_slots.at[0],
            dst_ref=peak_slots.at[k],
            send_sem=peak_send_sem.at[k - 1],
            recv_sem=peak_recv_sem.at[k - 1],
            device_id={"mkt": lax.rem(my_mkt + k, chips)},
            device_id_type=MESH,
        )

    wait_mkt(relay_sem.at[hops - 1], (-(2 << hops - 1), 2 << hops - 1))
    for k in range(1, chips):
        peak_copy(k).start()

    def choose(values):
        chosen = values[0]
        for g in range(1, draws):
            chosen = jnp.where(my_draw == g, values[g], chosen)
        return chosen

    ls_own = choose(ls)
    mean_own = choose(means)
    change = choose(changes)
    count_own = choose([packed(wide_counts, g * own) for g in range(draws)])
    valid_own = (product.astype(jnp.float32) < count_own) & (lane8 < tiles * own)

    for c in range(pieces):
        for k in distant:
            fill(k, c)

    def largest_of(slots_ref):
        rows = [slots_ref[n] for n in range(slots_ref.shape[0])]
        while len(rows) > 1:
            rows = [
                jnp.maximum(rows[n], rows[n + 1]) if n + 1 < len(rows) else rows[n]
                for n in range(0, len(rows), 2)
            ]
        return jnp.max(rows[0], axis=1, keepdims=True)

    def step_of(largest):
        return jnp.minimum(1.0, step_cap / (largest + epsilon))

    for k in range(1, chips):
        peak_copy(k).wait_recv()
    norms = largest_of(peak_slots)
    mean_own = mean_own + step_of(norms) * change

    lanes_of = [slice(at, at + LANES) for at in range(0, draws * consumers, LANES)]

    def denominators(weight):
        for m in range(own):
            column = jnp.concatenate(
                [weight[:, t * own + m : t * own + m + 1] for t in range(tiles)], axis=0
            )
            for n, chunk in enumerate(lanes_of):
                inverse_ref[m, n : n + 1, :] = 1.0 + jnp.sum(
                    column * held[m, :, chunk], axis=0, keepdims=True
                )
        inverse_ref[...] = 1.0 / inverse_ref[...]

    def sweep(weight):
        denominators(weight)
        part = jnp.zeros((8, LANES), jnp.float32)
        for m in range(own):
            column = None
            for n, chunk in enumerate(lanes_of):
                term = held[m, :, chunk] * inverse_ref[m, n : n + 1, :]
                column = term if column is None else column + term
            part = placed(part, jnp.sum(column, axis=1, keepdims=True), m)
        return part

    others = [(m, d) for m in range(chips) for d in range(draws) if m or d]

    def peaks_copy(it, n):
        m, d = others[n]
        return pltpu.make_async_remote_copy(
            src_ref=peaks_slots.at[it, 0],
            dst_ref=peaks_slots.at[it, n + 1],
            send_sem=peaks_send_sem.at[it],
            recv_sem=peaks_recv_sem.at[it],
            device_id={
                "mkt": lax.rem(my_mkt + m, chips),
                "draw": lax.rem(my_draw + d, draws),
            },
            device_id_type=MESH,
        )

    def peaks_all(it, sem):
        span = peaks_slots.at[it, pl.ds(1, len(others))]
        return pltpu.make_async_copy(span, span, sem.at[it])

    def mean_copy(k):
        return pltpu.make_async_remote_copy(
            src_ref=mean_slots.at[my_draw],
            dst_ref=mean_slots.at[my_draw],
            send_sem=mean_send_sem.at[k - 1],
            recv_sem=mean_recv_sem.at[k - 1],
            device_id={"draw": lax.rem(my_draw + k, draws)},
            device_id_type=MESH,
        )

    norms_ref[0] = norms
    def iteration(it, mean_own):
        weight = jnp.where(valid_own, jnp.exp(mean_own), 0.0)
        change = change_of(weight, sweep(weight), ls_own, valid_own)
        peaks_slots[it, 0] = jnp.max(jnp.abs(change), axis=0, keepdims=True)
        for n in range(len(others)):
            peaks_copy(it, n).start()

        @pl.when(it == ITERS - 2)
        def _():
            mean_slots[my_draw, 0] = mean_own
            mean_slots[my_draw, 1] = change
            for k in range(1, draws):
                mean_copy(k).start()

        peaks_all(it, peaks_recv_sem).wait()
        largest = largest_of(peaks_slots.at[it])
        norms_ref[it + 1] = largest
        return mean_own + step_of(largest) * change

    mean_own = lax.fori_loop(0, ITERS - 1, iteration, mean_own)

    for k in range(1, draws):
        mean_copy(k).wait_recv()
    step = step_of(norms_ref[ITERS - 1])
    mean_tiles = [mean_slots[d, 0] + step * mean_slots[d, 1] for d in range(draws)]
    for t in range(tiles):
        total = mean_tiles[0]
        total = pltpu.roll(total, LANES - t * own, 1) if t else total
        for d in range(1, draws):
            shift = (d - t) * own % LANES
            moved = pltpu.roll(mean_tiles[d], shift, 1) if shift else mean_tiles[d]
            total = jnp.where(lane8 >= d * own, moved, total)
        square[8 * t : 8 * t + 8, :] = total
    mean_rows = square[...].T
    mean_out[...] = mean_rows[0:markets, 0:slots]
    rows_ref[...] = jnp.exp(mean_rows[0:markets])

    weight = jnp.where(valid_own, jnp.exp(mean_own), 0.0)
    eye = jnp.where(row == lane, 1.0, 0.0)
    ones = jnp.ones((8, draws * consumers), jnp.float32)
    scale = jnp.where(lane < slots, 0.5, 1.0)

    denominators(weight)

    def last_sweep(b, carry):
        sums = []
        for u in range(block):
            chance = jnp.concatenate(
                [
                    held[b * block + u, :, chunk] * inverse_ref[b * block + u, n : n + 1, :]
                    for n, chunk in enumerate(lanes_of)
                ],
                axis=1,
            )
            low = chance - rounded(chance)
            left = jnp.concatenate([chance, low], axis=0).astype(jnp.bfloat16)
            right = jnp.concatenate([chance, ones], axis=0).astype(jnp.bfloat16)
            products = lax.dot_general(
                left, right, (((1,), (1,)), ((), ())), preferred_element_type=jnp.float32
            )
            products = jnp.concatenate(
                [products, jnp.zeros((2 * slots, LANES - slots - 8), jnp.float32)], axis=1
            )
            sums.append(scale * products[0:slots] + products[slots:])
        for at in range(0, block, 2):
            pair = sums[at]
            if at + 1 < block:
                pair = jnp.where(lane < half, pair, pltpu.roll(sums[at + 1], half, 1))
            turn[at // 2 * half : at // 2 * half + slots, :] = pair
        turn[...] = turn[...].T
        for u in range(block):
            other = turn[u % 2 * half : u % 2 * half + slots, :]
            other = pltpu.roll(other, half, 1) if u // 2 else other
            m = b * block + u
            count = counts_ref[my_draw * own + m]
            here = (row < count) & (lane < count)
            ratio = (sums[u] + other) * rows_ref[pl.ds(my_draw * own + m, 1), :]
            ratio = ratio * (1.0 / sums[u][:, slots : slots + 1])
            jac_out[m] = jnp.where(here, eye - ratio, 0.0)[:, 0:slots]
        return carry

    lax.fori_loop(0, own // block, last_sweep, 0, unroll=True)

    for it in range(ITERS):
        norms_out[it] = norms_ref[it][0, 0]
    for k in range(1, draws):
        mean_copy(k).wait_send()
        for c in range(pieces):
            far_copy(k, c).wait_send()
        for g in range(1, draws + 1):
            part_copy(k, g).wait_send()
    for k in range(1, chips):
        peak_copy(k).wait_send()
    for it in range(ITERS - 1):
        peaks_all(it, peaks_send_sem).wait()


def store(mean, jac, norms, mean_out, jac_out, norms_out, sem):
    copies = [
        pltpu.make_async_copy(source, target, sem.at[n])
        for n, (source, target) in enumerate(
            ((jac, jac_out), (mean, mean_out), (norms, norms_out))
        )
    ]
    for copy in copies:
        copy.start()
    for copy in copies:
        copy.wait()


def shards(x_char, nu_draws, coef_sigma, log_share, counts):
    markets, slots, coefs = x_char.shape
    consumers = nu_draws.shape[2]
    draws, chips = lax.axis_size("draw"), lax.axis_size("mkt")
    own = markets // draws
    pieces = divisor_up_to(own, PIECES)
    vmem = pl.BlockSpec(memory_space=pltpu.VMEM)
    smem = pl.BlockSpec(memory_space=pltpu.SMEM)
    f32 = jnp.float32
    dma = pltpu.SemaphoreType.DMA
    results = pl.pallas_call(
        functools.partial(kernel, draws, chips, 1.0 / (consumers * draws)),
        out_shape=(
            jax.ShapeDtypeStruct((markets, slots), f32),
            jax.ShapeDtypeStruct((own, slots, slots), f32),
            jax.ShapeDtypeStruct((ITERS,), f32),
        ),
        in_specs=[pl.BlockSpec(memory_space=pltpu.HBM)] * 6,
        out_specs=(vmem, vmem, smem),
        scratch_shapes=[
            pltpu.SMEM((coefs,), f32),
            pltpu.SMEM((markets,), jnp.int32),
            pltpu.VMEM((1, markets), jnp.int32),
            pltpu.VMEM((markets, slots), f32),
            pltpu.VMEM((markets, coefs, slots), f32),
            pltpu.VMEM((draws, own, coefs, consumers), f32),
            pltpu.VMEM((draws - 1, own, coefs, consumers), f32),
            pltpu.VMEM((own, slots, draws * consumers), f32),
            pltpu.VMEM((own, consumers), f32),
            pltpu.VMEM((own, draws * consumers // LANES, LANES), f32),
            pltpu.VMEM((markets, LANES), f32),
            pltpu.VMEM((LANES, LANES), f32),
            pltpu.VMEM((LANES, LANES), f32),
            pltpu.VMEM((ITERS, 1, 1), f32),
            pltpu.VMEM((draws, draws, 8, LANES), f32),
            pltpu.VMEM((chips, 1, LANES), f32),
            pltpu.VMEM((ITERS - 1, chips * draws, 1, LANES), f32),
            pltpu.VMEM((draws, 2, 8, LANES), f32),
            dma((draws - 1, draws)),
            dma((draws - 1, draws)),
            dma((chips,)),
            dma((chips,)),
            dma((ITERS - 1,)),
            dma((ITERS - 1,)),
            dma((draws - 1, pieces)),
            dma((draws - 1, pieces)),
            dma((draws,)),
            dma((draws,)),
            pltpu.SemaphoreType.REGULAR((max(1, (chips - 1).bit_length() - 1),)),
            dma((5,)),
            dma((draws,)),
        ],
        compiler_params=pltpu.CompilerParams(
            collective_id=0, has_side_effects=True, vmem_limit_bytes=VMEM_LIMIT
        ),
        name="contraction",
    )(
        *(
            pltpu.with_memory_space_constraint(operand, pltpu.HBM)
            for operand in (
                coef_sigma,
                counts,
                counts[None, :],
                log_share,
                jnp.swapaxes(x_char, 1, 2),
                nu_draws,
            )
        )
    )
    hbm = pl.BlockSpec(memory_space=pltpu.HBM)
    return pl.pallas_call(
        store,
        out_shape=tuple(jax.ShapeDtypeStruct(r.shape, r.dtype) for r in results),
        in_specs=[vmem, vmem, vmem],
        out_specs=(hbm, hbm, hbm),
        scratch_shapes=[dma((3,))],
        name="store",
    )(*(pltpu.with_memory_space_constraint(r, pltpu.VMEM) for r in results))


def solution(mesh):
    return jax.shard_map(
        shards,
        mesh=mesh,
        in_specs=(P("mkt", None, None), P("mkt", None, "draw"), P(), P("mkt", None), P("mkt")),
        out_specs=(P("mkt", None), P(("mkt", "draw"), None, None), P()),
        check_vma=False,
    )
```

```python
import functools
import math

import jax
import jax.numpy as jnp
from jax import lax
from jax.experimental import pallas as pl
from jax.experimental.pallas import tpu as pltpu
from jax.sharding import PartitionSpec as P

ITERS = 3
LANES = 128
BLOCK = 4
PIECES = 4
EARLY = 1
VMEM_LIMIT = 48 * 1024 * 1024
MESH = pl.DeviceIdType.MESH

step_cap = 0.25
epsilon = 1e-06


def divisor_up_to(count, most):
    return max(size for size in range(1, most + 1) if count % size == 0)


def rounded(value):
    return value.astype(jnp.bfloat16).astype(jnp.float32)


def split2(value):
    first = rounded(value)
    return first, value - first


def kernel(
    draws,
    chips,
    inverse,
    sigma_hbm,
    counts_hbm,
    counts_row_hbm,
    log_share_hbm,
    x_hbm,
    nu_hbm,
    mean_out,
    jac_out,
    norms_out,
    sigma_ref,
    counts_ref,
    counts_row_ref,
    log_share_ref,
    x_ref,
    nu_ref,
    far_ref,
    held,
    first_ref,
    inverse_ref,
    partial_ref,
    ls_ref,
    mean_ref,
    change_ref,
    weight_ref,
    rows_ref,
    square,
    turn,
    norms_ref,
    part_slots,
    peak_slots,
    peaks_slots,
    mean_slots,
    part_send_sem,
    part_recv_sem,
    peak_send_sem,
    peak_recv_sem,
    peaks_send_sem,
    peaks_recv_sem,
    far_send_sem,
    far_recv_sem,
    mean_send_sem,
    mean_recv_sem,
    relay_sem,
    load_sem,
    nu_sem,
):
    markets, coefs, slots = x_ref.shape
    own = markets // draws
    consumers = nu_ref.shape[3]
    tiles = slots // 8
    half = LANES // 2
    block = divisor_up_to(own, BLOCK)
    pieces = far_send_sem.shape[1]
    piece = own // pieces
    my_draw = lax.axis_index("draw")
    my_mkt = lax.axis_index("mkt")
    cores = 2 if draws % 2 == 0 else 1

    def partner(k):
        chip = (my_draw // cores + (k - 1) // cores + 1) % (draws // cores)
        core = (my_draw + k) % cores
        return chip * cores + core

    loads = [
        pltpu.make_async_copy(source, target, load_sem.at[n])
        for n, (source, target) in enumerate(
            (
                (counts_row_hbm, counts_row_ref),
                (log_share_hbm, log_share_ref),
                (sigma_hbm, sigma_ref),
                (counts_hbm, counts_ref),
                (x_hbm, x_ref),
            )
        )
    ]

    def nu_load(k):
        return pltpu.make_async_copy(
            nu_hbm.at[pl.ds(partner(k) * own, own)], nu_ref.at[k - 1], nu_sem.at[k - 1]
        )

    for load in loads:
        load.start()
    for k in range(1, draws + 1):
        nu_load(k).start()

    barrier = pltpu.get_barrier_semaphore()
    for k in range(1, draws):
        pl.semaphore_signal(
            barrier, inc=1, device_id={"draw": lax.rem(my_draw + k, draws)}, device_id_type=MESH
        )

    def beside(k):
        return (my_mkt + k >= 0) & (my_mkt + k < chips)

    def signal_mkt(sem, spans):
        for k in spans:

            @pl.when(beside(k))
            def _(k=k):
                pl.semaphore_signal(
                    sem, inc=1, device_id={"mkt": my_mkt + k}, device_id_type=MESH
                )

    def wait_mkt(sem, spans, more=0):
        count = more
        for k in spans:
            count = count + jnp.where(beside(k), 1, 0)
        pl.semaphore_wait(sem, count)

    spans = [k for k in (-2, -1, 1, 2) if abs(k) < chips]
    signal_mkt(barrier, spans)

    def far_copy(k, c):
        return pltpu.make_async_remote_copy(
            src_ref=nu_hbm.at[pl.ds(partner(k) * own + c * piece, piece)],
            dst_ref=far_ref.at[k - 1, pl.ds(c * piece, piece)],
            send_sem=far_send_sem.at[k - 1, c],
            recv_sem=far_recv_sem.at[k - 1, c],
            device_id={"draw": partner(k)},
            device_id_type=MESH,
        )

    near = range(max(1, draws - cores + 1), draws)
    distant = range(1, max(1, draws - cores + 1))

    lane = lax.broadcasted_iota(jnp.int32, (slots, LANES), 1)
    row = lax.broadcasted_iota(jnp.int32, (slots, LANES), 0)
    lane8 = lax.broadcasted_iota(jnp.int32, (8, LANES), 1)
    row8 = lax.broadcasted_iota(jnp.int32, (8, LANES), 0)

    wait_mkt(barrier, spans, draws - 1)
    for c in range(min(EARLY, pieces)):
        for k in distant:
            far_copy(k, c).start()
    for k in near:
        for c in range(pieces):
            far_copy(k, c).start()
    hops = relay_sem.shape[0]
    signal_mkt(relay_sem.at[0], (-2, 2))

    square[...] = jnp.zeros_like(square)
    for load in loads:
        load.wait()
    square[0:markets, 0:slots] = log_share_ref[...]
    log_share = square[...].T[0:slots, :]
    square[0:1, 0:markets] = counts_row_ref[...].astype(jnp.float32)
    counts = square[0:1, :]
    usable = (row.astype(jnp.float32) < counts) & (lane < markets)
    inside = jnp.sum(jnp.where(usable, jnp.exp(log_share), 0.0), axis=0, keepdims=True)
    mean = jnp.where(usable, log_share - jnp.log(1.0 - inside), 0.0)
    weights = jnp.where(usable, jnp.exp(mean), 0.0)

    coef_row = lax.broadcasted_iota(jnp.int32, (coefs, slots), 0)
    sigma = jnp.zeros((coefs, slots), jnp.float32)
    for k in range(coefs):
        sigma = jnp.where(coef_row == k, sigma_ref[k] * math.log2(math.e), sigma)

    def raised_tastes(chars, draw):
        s1, s2 = split2(chars * sigma)
        n1, n2 = split2(draw)
        left = jnp.concatenate([s1, s1, s2, s2], axis=0).astype(jnp.bfloat16)
        right = jnp.concatenate([n1, n2, n1, n2], axis=0).astype(jnp.bfloat16)
        tastes = lax.dot_general(
            left, right, (((0,), (0,)), ((), ())), preferred_element_type=jnp.float32
        )
        return jnp.exp2(tastes)

    def packed(value, base):
        total = jnp.zeros((8, LANES), jnp.float32)
        for t in range(tiles):
            shift = (t * own - base) % LANES
            moved = value[8 * t : 8 * t + 8]
            moved = pltpu.roll(moved, shift, 1) if shift else moved
            total = jnp.where((lane8 >= t * own) & (lane8 < (t + 1) * own), moved, total)
        return total

    def placed(part, column, i):
        for t in range(tiles):
            part = jnp.where(lane8 == t * own + i, column[8 * t : 8 * t + 8], part)
        return part

    def part_copy(k, g):
        return pltpu.make_async_remote_copy(
            src_ref=part_slots.at[my_draw, partner(g)],
            dst_ref=part_slots.at[my_draw, partner(g)],
            send_sem=part_send_sem.at[k - 1, g - 1],
            recv_sem=part_recv_sem.at[k - 1, g - 1],
            device_id={"draw": lax.rem(my_draw + k, draws)},
            device_id_type=MESH,
        )

    mine = (draws - 1) * consumers
    near_chunks = [
        slice(at, min(at + LANES, consumers)) for at in range(0, consumers, LANES)
    ]

    def first_sweep(g, carry):
        base = partner(g) * own
        nu_load(g).wait()
        local = pltpu.roll(weights, lax.rem(LANES - base, LANES), 1)
        for i in range(own):
            weight = local[:, i : i + 1]
            known = raised_tastes(x_ref[base + i], nu_ref[g - 1, i])
            held[i, :, mine : mine + consumers] = known
            for chunk in near_chunks:
                first_ref[i : i + 1, chunk] = 1.0 + jnp.sum(
                    weight * known[:, chunk], axis=0, keepdims=True
                )
        first_ref[...] = 1.0 / first_ref[...]
        part = jnp.zeros((8, LANES), jnp.float32)
        for i in range(own):
            column = None
            for chunk in near_chunks:
                term = (
                    held[i, :, mine + chunk.start : mine + chunk.stop]
                    * first_ref[i : i + 1, chunk]
                )
                column = term if column is None else column + term
            part = placed(part, jnp.sum(column, axis=1, keepdims=True), i)
        part_slots[my_draw, partner(g)] = part
        for k in range(1, draws):
            part_copy(k, g).start()
        return carry

    lax.fori_loop(1, draws + 1, first_sweep, 0)

    for c in range(min(EARLY, pieces), pieces):
        for k in distant:
            far_copy(k, c).start()
    for hop in range(hops - 1):
        reach = 2 << hop
        wait_mkt(relay_sem.at[hop], (-reach, reach))
        signal_mkt(relay_sem.at[hop + 1], (-2 * reach, 2 * reach))

    def fill(k, c):
        far_copy(k, c).wait_recv()

        def body(i, carry):
            m = c * piece + i
            held[m, :, (k - 1) * consumers : k * consumers] = raised_tastes(
                x_ref[my_draw * own + m], far_ref[k - 1, m]
            )
            return carry

        lax.fori_loop(0, piece, body, 0, unroll=True)

    for c in range(pieces):
        for k in near:
            fill(k, c)

    product = row8
    for t in range(1, tiles):
        product = jnp.where(lane8 >= t * own, row8 + 8 * t, product)
    wide_counts = jnp.broadcast_to(counts, (slots, LANES))
    ls, means, valid = [], [], []
    for g in range(draws):
        ls.append(packed(log_share, g * own))
        means.append(packed(mean, g * own))
        valid.append(
            (product.astype(jnp.float32) < packed(wide_counts, g * own)) & (lane8 < tiles * own)
        )

    def change_of(weight, total, ls, valid):
        shares = jnp.where(valid, weight * total * inverse, 1.0)
        return jnp.where(valid, ls - jnp.log(shares), 0.0)

    def choose(values):
        chosen = values[0]
        for g in range(1, draws):
            chosen = jnp.where(my_draw == g, values[g], chosen)
        return chosen

    def spread(target, value):
        for m in range(own):
            for t in range(tiles):
                target[m, 8 * t : 8 * t + 8, :] = jnp.broadcast_to(
                    value[:, t * own + m : t * own + m + 1], (8, LANES)
                )

    spread(ls_ref, choose(ls))
    spread(mean_ref, choose(means))

    start_weights = [jnp.where(valid[g], jnp.exp(means[g]), 0.0) for g in range(draws)]
    for g in range(1, draws + 1):
        for k in range(1, draws):
            part_copy(k, g).wait_recv()
    changes = []
    peak = jnp.zeros((8, LANES), jnp.float32)
    for g in range(draws):
        total = part_slots[0, g]
        for d in range(1, draws):
            total = total + part_slots[d, g]
        changes.append(change_of(start_weights[g], total, ls[g], valid[g]))
        peak = jnp.maximum(peak, jnp.abs(changes[g]))
    peak_slots[0] = jnp.max(peak, axis=0, keepdims=True)

    def peak_copy(k):
        return pltpu.make_async_remote_copy(
            src_ref=peak_slots.at[0],
            dst_ref=peak_slots.at[k],
            send_sem=peak_send_sem.at[k - 1],
            recv_sem=peak_recv_sem.at[k - 1],
            device_id={"mkt": lax.rem(my_mkt + k, chips)},
            device_id_type=MESH,
        )

    wait_mkt(relay_sem.at[hops - 1], (-(2 << hops - 1), 2 << hops - 1))
    for k in range(1, chips):
        peak_copy(k).start()

    spread(change_ref, choose(changes))

    for c in range(pieces):
        for k in distant:
            fill(k, c)

    def largest_of(slots_ref):
        rows = [slots_ref[n] for n in range(slots_ref.shape[0])]
        while len(rows) > 1:
            rows = [
                jnp.maximum(rows[n], rows[n + 1]) if n + 1 < len(rows) else rows[n]
                for n in range(0, len(rows), 2)
            ]
        return jnp.max(rows[0], axis=1, keepdims=True)

    def step_of(largest):
        return jnp.minimum(1.0, step_cap / (largest + epsilon))

    for k in range(1, chips):
        peak_copy(k).wait_recv()
    largest = largest_of(peak_slots)
    norms_ref[0] = largest

    lanes_of = [slice(at, at + LANES) for at in range(0, draws * consumers, LANES)]

    def count_of(m):
        return counts_ref[my_draw * own + m]

    def denominators(step):
        for m in range(own):
            mean = mean_ref[m] + step * change_ref[m]
            mean_ref[m] = mean
            weight = jnp.where(row < count_of(m), jnp.exp(mean), 0.0)
            weight_ref[m] = weight
            for n, chunk in enumerate(lanes_of):
                raised = weight * held[m, :, chunk]
                total = raised[0:8]
                for t in range(1, tiles):
                    total = total + raised[8 * t : 8 * t + 8]
                partial_ref[m, 8 * n : 8 * n + 8, :] = total
            total = partial_ref[m, pl.ds(0, len(lanes_of), stride=8), :]
            for t in range(1, 8):
                total = total + partial_ref[m, pl.ds(t, len(lanes_of), stride=8), :]
            inverse_ref[m] = 1.0 / (1.0 + total)

    def sweep(step):
        denominators(step)
        peak = jnp.zeros((8, LANES), jnp.float32)
        for m in range(own):
            column = None
            for n, chunk in enumerate(lanes_of):
                term = held[m, :, chunk] * inverse_ref[m, n : n + 1, :]
                column = term if column is None else column + term
            total = jnp.sum(column, axis=1, keepdims=True)
            change = change_of(weight_ref[m], total, ls_ref[m], row < count_of(m))
            change_ref[m] = change
            for t in range(tiles):
                peak = jnp.maximum(peak, jnp.abs(change[8 * t : 8 * t + 8]))
        return jnp.max(peak, axis=0, keepdims=True)

    def gathered(source):
        tile = jnp.zeros((8, LANES), jnp.float32)
        for m in range(own):
            tile = placed(tile, source[m], m)
        return tile

    others = [(m, d) for m in range(chips) for d in range(draws) if m or d]

    def peaks_copy(it, n):
        m, d = others[n]
        return pltpu.make_async_remote_copy(
            src_ref=peaks_slots.at[it, 0],
            dst_ref=peaks_slots.at[it, n + 1],
            send_sem=peaks_send_sem.at[it],
            recv_sem=peaks_recv_sem.at[it],
            device_id={
                "mkt": lax.rem(my_mkt + m, chips),
                "draw": lax.rem(my_draw + d, draws),
            },
            device_id_type=MESH,
        )

    def peaks_all(it, sem):
        span = peaks_slots.at[it, pl.ds(1, len(others))]
        return pltpu.make_async_copy(span, span, sem.at[it])

    def mean_copy(k):
        return pltpu.make_async_remote_copy(
            src_ref=mean_slots.at[my_draw],
            dst_ref=mean_slots.at[my_draw],
            send_sem=mean_send_sem.at[k - 1],
            recv_sem=mean_recv_sem.at[k - 1],
            device_id={"draw": lax.rem(my_draw + k, draws)},
            device_id_type=MESH,
        )

    def iteration(it, step):
        peaks_slots[it, 0] = sweep(step)
        for n in range(len(others)):
            peaks_copy(it, n).start()

        @pl.when(it == ITERS - 2)
        def _():
            mean_slots[my_draw, 0] = gathered(mean_ref)
            mean_slots[my_draw, 1] = gathered(change_ref)
            for k in range(1, draws):
                mean_copy(k).start()

        peaks_all(it, peaks_recv_sem).wait()
        largest = largest_of(peaks_slots.at[it])
        norms_ref[it + 1] = largest
        return step_of(largest)

    step = lax.fori_loop(0, ITERS - 1, iteration, step_of(largest))

    for k in range(1, draws):
        mean_copy(k).wait_recv()
    mean_tiles = [mean_slots[d, 0] + step * mean_slots[d, 1] for d in range(draws)]
    for t in range(tiles):
        total = mean_tiles[0]
        total = pltpu.roll(total, LANES - t * own, 1) if t else total
        for d in range(1, draws):
            shift = (d - t) * own % LANES
            moved = pltpu.roll(mean_tiles[d], shift, 1) if shift else mean_tiles[d]
            total = jnp.where(lane8 >= d * own, moved, total)
        square[8 * t : 8 * t + 8, :] = total
    mean_rows = square[...].T
    mean_out[...] = mean_rows[0:markets, 0:slots]
    rows_ref[...] = jnp.exp(mean_rows[0:markets])

    eye = jnp.where(row == lane, 1.0, 0.0)
    ones = jnp.ones((8, draws * consumers), jnp.float32)
    scale = jnp.where(lane < slots, 0.5, 1.0)

    denominators(step)

    def last_sweep(b, carry):
        sums = []
        for u in range(block):
            chance = jnp.concatenate(
                [
                    held[b * block + u, :, chunk] * inverse_ref[b * block + u, n : n + 1, :]
                    for n, chunk in enumerate(lanes_of)
                ],
                axis=1,
            )
            low = chance - rounded(chance)
            left = jnp.concatenate([chance, low], axis=0).astype(jnp.bfloat16)
            right = jnp.concatenate([chance, ones], axis=0).astype(jnp.bfloat16)
            products = lax.dot_general(
                left, right, (((1,), (1,)), ((), ())), preferred_element_type=jnp.float32
            )
            products = jnp.concatenate(
                [products, jnp.zeros((2 * slots, LANES - slots - 8), jnp.float32)], axis=1
            )
            sums.append(scale * products[0:slots] + products[slots:])
        for at in range(0, block, 2):
            pair = sums[at]
            if at + 1 < block:
                pair = jnp.where(lane < half, pair, pltpu.roll(sums[at + 1], half, 1))
            turn[at // 2 * half : at // 2 * half + slots, :] = pair
        turn[...] = turn[...].T
        for u in range(block):
            other = turn[u % 2 * half : u % 2 * half + slots, :]
            other = pltpu.roll(other, half, 1) if u // 2 else other
            m = b * block + u
            count = counts_ref[my_draw * own + m]
            here = (row < count) & (lane < count)
            ratio = (sums[u] + other) * rows_ref[pl.ds(my_draw * own + m, 1), :]
            ratio = ratio * (1.0 / sums[u][:, slots : slots + 1])
            jac_out[m] = jnp.where(here, eye - ratio, 0.0)[:, 0:slots]
        return carry

    lax.fori_loop(0, own // block, last_sweep, 0, unroll=True)

    for it in range(ITERS):
        norms_out[it] = norms_ref[it][0, 0]
    for k in range(1, draws):
        mean_copy(k).wait_send()
        for c in range(pieces):
            far_copy(k, c).wait_send()
        for g in range(1, draws + 1):
            part_copy(k, g).wait_send()
    for k in range(1, chips):
        peak_copy(k).wait_send()
    for it in range(ITERS - 1):
        peaks_all(it, peaks_send_sem).wait()


def store(mean, jac, norms, mean_out, jac_out, norms_out, sem):
    copies = [
        pltpu.make_async_copy(source, target, sem.at[n])
        for n, (source, target) in enumerate(
            ((jac, jac_out), (mean, mean_out), (norms, norms_out))
        )
    ]
    for copy in copies:
        copy.start()
    for copy in copies:
        copy.wait()


def shards(x_char, nu_draws, coef_sigma, log_share, counts):
    markets, slots, coefs = x_char.shape
    consumers = nu_draws.shape[2]
    draws, chips = lax.axis_size("draw"), lax.axis_size("mkt")
    own = markets // draws
    pieces = divisor_up_to(own, PIECES)
    vmem = pl.BlockSpec(memory_space=pltpu.VMEM)
    smem = pl.BlockSpec(memory_space=pltpu.SMEM)
    f32 = jnp.float32
    dma = pltpu.SemaphoreType.DMA
    results = pl.pallas_call(
        functools.partial(kernel, draws, chips, 1.0 / (consumers * draws)),
        out_shape=(
            jax.ShapeDtypeStruct((markets, slots), f32),
            jax.ShapeDtypeStruct((own, slots, slots), f32),
            jax.ShapeDtypeStruct((ITERS,), f32),
        ),
        in_specs=[pl.BlockSpec(memory_space=pltpu.HBM)] * 6,
        out_specs=(vmem, vmem, smem),
        scratch_shapes=[
            pltpu.SMEM((coefs,), f32),
            pltpu.SMEM((markets,), jnp.int32),
            pltpu.VMEM((1, markets), jnp.int32),
            pltpu.VMEM((markets, slots), f32),
            pltpu.VMEM((markets, coefs, slots), f32),
            pltpu.VMEM((draws, own, coefs, consumers), f32),
            pltpu.VMEM((draws - 1, own, coefs, consumers), f32),
            pltpu.VMEM((own, slots, draws * consumers), f32),
            pltpu.VMEM((own, consumers), f32),
            pltpu.VMEM((own, draws * consumers // LANES, LANES), f32),
            pltpu.VMEM((own, draws * consumers // LANES * 8, LANES), f32),
            pltpu.VMEM((own, slots, LANES), f32),
            pltpu.VMEM((own, slots, LANES), f32),
            pltpu.VMEM((own, slots, LANES), f32),
            pltpu.VMEM((own, slots, LANES), f32),
            pltpu.VMEM((markets, LANES), f32),
            pltpu.VMEM((LANES, LANES), f32),
            pltpu.VMEM((LANES, LANES), f32),
            pltpu.VMEM((ITERS, 1, 1), f32),
            pltpu.VMEM((draws, draws, 8, LANES), f32),
            pltpu.VMEM((chips, 1, LANES), f32),
            pltpu.VMEM((ITERS - 1, chips * draws, 1, LANES), f32),
            pltpu.VMEM((draws, 2, 8, LANES), f32),
            dma((draws - 1, draws)),
            dma((draws - 1, draws)),
            dma((chips,)),
            dma((chips,)),
            dma((ITERS - 1,)),
            dma((ITERS - 1,)),
            dma((draws - 1, pieces)),
            dma((draws - 1, pieces)),
            dma((draws,)),
            dma((draws,)),
            pltpu.SemaphoreType.REGULAR((max(1, (chips - 1).bit_length() - 1),)),
            dma((5,)),
            dma((draws,)),
        ],
        compiler_params=pltpu.CompilerParams(
            collective_id=0, has_side_effects=True, vmem_limit_bytes=VMEM_LIMIT
        ),
        name="contraction",
    )(
        *(
            pltpu.with_memory_space_constraint(operand, pltpu.HBM)
            for operand in (
                coef_sigma,
                counts,
                counts[None, :],
                log_share,
                jnp.swapaxes(x_char, 1, 2),
                nu_draws,
            )
        )
    )
    hbm = pl.BlockSpec(memory_space=pltpu.HBM)
    return pl.pallas_call(
        store,
        out_shape=tuple(jax.ShapeDtypeStruct(r.shape, r.dtype) for r in results),
        in_specs=[vmem, vmem, vmem],
        out_specs=(hbm, hbm, hbm),
        scratch_shapes=[dma((3,))],
        name="store",
    )(*(pltpu.with_memory_space_constraint(r, pltpu.VMEM) for r in results))


def solution(mesh):
    return jax.shard_map(
        shards,
        mesh=mesh,
        in_specs=(P("mkt", None, None), P("mkt", None, "draw"), P(), P("mkt", None), P("mkt")),
        out_specs=(P("mkt", None), P(("mkt", "draw"), None, None), P()),
        check_vma=False,
    )
```

```python
import functools
import math

import jax
import jax.numpy as jnp
from jax import lax
from jax.experimental import pallas as pl
from jax.experimental.pallas import tpu as pltpu
from jax.sharding import PartitionSpec as P

ITERS = 3
LANES = 128
BLOCK = 4
PIECES = 4
EARLY = 1
VMEM_LIMIT = 48 * 1024 * 1024
MESH = pl.DeviceIdType.MESH

step_cap = 0.25
epsilon = 1e-06


def divisor_up_to(count, most):
    return max(size for size in range(1, most + 1) if count % size == 0)


def rounded(value):
    return value.astype(jnp.bfloat16).astype(jnp.float32)


def split2(value):
    first = rounded(value)
    return first, value - first


def kernel(
    draws,
    chips,
    inverse,
    sigma_hbm,
    counts_hbm,
    counts_row_hbm,
    log_share_hbm,
    x_hbm,
    nu_hbm,
    mean_out,
    jac_out,
    norms_out,
    sigma_ref,
    counts_ref,
    counts_row_ref,
    log_share_ref,
    x_ref,
    nu_ref,
    far_ref,
    held,
    first_ref,
    inverse_ref,
    partial_ref,
    ls_ref,
    mean_ref,
    change_ref,
    weight_ref,
    rows_ref,
    square,
    turn,
    norms_ref,
    part_slots,
    peak_slots,
    peaks_slots,
    mean_slots,
    part_send_sem,
    part_recv_sem,
    peak_send_sem,
    peak_recv_sem,
    peaks_send_sem,
    peaks_recv_sem,
    far_send_sem,
    far_recv_sem,
    mean_send_sem,
    mean_recv_sem,
    relay_sem,
    load_sem,
    nu_sem,
):
    markets, coefs, slots = x_ref.shape
    own = markets // draws
    consumers = nu_ref.shape[3]
    tiles = slots // 8
    half = LANES // 2
    block = divisor_up_to(own, BLOCK)
    pieces = far_send_sem.shape[1]
    piece = own // pieces
    my_draw = lax.axis_index("draw")
    my_mkt = lax.axis_index("mkt")
    cores = 2 if draws % 2 == 0 else 1

    def partner(k):
        chip = (my_draw // cores + (k - 1) // cores + 1) % (draws // cores)
        core = (my_draw + k) % cores
        return chip * cores + core

    loads = [
        pltpu.make_async_copy(source, target, load_sem.at[n])
        for n, (source, target) in enumerate(
            (
                (counts_row_hbm, counts_row_ref),
                (log_share_hbm, log_share_ref),
                (sigma_hbm, sigma_ref),
                (counts_hbm, counts_ref),
                (x_hbm, x_ref),
            )
        )
    ]

    def nu_load(k):
        return pltpu.make_async_copy(
            nu_hbm.at[pl.ds(partner(k) * own, own)], nu_ref.at[k - 1], nu_sem.at[k - 1]
        )

    barrier = pltpu.get_barrier_semaphore()
    for k in range(1, draws):
        pl.semaphore_signal(
            barrier, inc=1, device_id={"draw": lax.rem(my_draw + k, draws)}, device_id_type=MESH
        )

    def beside(k):
        return (my_mkt + k >= 0) & (my_mkt + k < chips)

    def signal_mkt(sem, spans):
        for k in spans:

            @pl.when(beside(k))
            def _(k=k):
                pl.semaphore_signal(
                    sem, inc=1, device_id={"mkt": my_mkt + k}, device_id_type=MESH
                )

    def wait_mkt(sem, spans, more=0):
        count = more
        for k in spans:
            count = count + jnp.where(beside(k), 1, 0)
        pl.semaphore_wait(sem, count)

    spans = [k for k in (-2, -1, 1, 2) if abs(k) < chips]
    for load in loads:
        load.start()
    for k in range(1, draws + 1):
        nu_load(k).start()
    signal_mkt(barrier, spans)

    def far_copy(k, c):
        return pltpu.make_async_remote_copy(
            src_ref=nu_hbm.at[pl.ds(partner(k) * own + c * piece, piece)],
            dst_ref=far_ref.at[k - 1, pl.ds(c * piece, piece)],
            send_sem=far_send_sem.at[k - 1, c],
            recv_sem=far_recv_sem.at[k - 1, c],
            device_id={"draw": partner(k)},
            device_id_type=MESH,
        )

    near = range(max(1, draws - cores + 1), draws)
    distant = range(1, max(1, draws - cores + 1))

    lane = lax.broadcasted_iota(jnp.int32, (slots, LANES), 1)
    row = lax.broadcasted_iota(jnp.int32, (slots, LANES), 0)
    lane8 = lax.broadcasted_iota(jnp.int32, (8, LANES), 1)
    row8 = lax.broadcasted_iota(jnp.int32, (8, LANES), 0)

    wait_mkt(barrier, spans, draws - 1)
    for c in range(min(EARLY, pieces)):
        for k in distant:
            far_copy(k, c).start()
    for k in near:
        for c in range(pieces):
            far_copy(k, c).start()
    hops = relay_sem.shape[0]
    signal_mkt(relay_sem.at[0], (-2, 2))

    square[...] = jnp.zeros_like(square)
    for load in loads:
        load.wait()
    square[0:markets, 0:slots] = log_share_ref[...]
    log_share = square[...].T[0:slots, :]
    square[0:1, 0:markets] = counts_row_ref[...].astype(jnp.float32)
    counts = square[0:1, :]
    usable = (row.astype(jnp.float32) < counts) & (lane < markets)
    inside = jnp.sum(jnp.where(usable, jnp.exp(log_share), 0.0), axis=0, keepdims=True)
    mean = jnp.where(usable, log_share - jnp.log(1.0 - inside), 0.0)
    weights = jnp.where(usable, jnp.exp(mean), 0.0)

    coef_row = lax.broadcasted_iota(jnp.int32, (coefs, slots), 0)
    sigma = jnp.zeros((coefs, slots), jnp.float32)
    for k in range(coefs):
        sigma = jnp.where(coef_row == k, sigma_ref[k] * math.log2(math.e), sigma)

    def raised_tastes(chars, draw):
        s1, s2 = split2(chars * sigma)
        n1, n2 = split2(draw)
        left = jnp.concatenate([s1, s1, s2, s2], axis=0).astype(jnp.bfloat16)
        right = jnp.concatenate([n1, n2, n1, n2], axis=0).astype(jnp.bfloat16)
        tastes = lax.dot_general(
            left, right, (((0,), (0,)), ((), ())), preferred_element_type=jnp.float32
        )
        return jnp.exp2(tastes)

    def packed(value, base):
        total = jnp.zeros((8, LANES), jnp.float32)
        for t in range(tiles):
            shift = (t * own - base) % LANES
            moved = value[8 * t : 8 * t + 8]
            moved = pltpu.roll(moved, shift, 1) if shift else moved
            total = jnp.where((lane8 >= t * own) & (lane8 < (t + 1) * own), moved, total)
        return total

    def placed(part, column, i):
        for t in range(tiles):
            part = jnp.where(lane8 == t * own + i, column[8 * t : 8 * t + 8], part)
        return part

    def part_copy(k, g):
        return pltpu.make_async_remote_copy(
            src_ref=part_slots.at[my_draw, partner(g)],
            dst_ref=part_slots.at[my_draw, partner(g)],
            send_sem=part_send_sem.at[k - 1, g - 1],
            recv_sem=part_recv_sem.at[k - 1, g - 1],
            device_id={"draw": lax.rem(my_draw + k, draws)},
            device_id_type=MESH,
        )

    mine = (draws - 1) * consumers
    near_chunks = [
        slice(at, min(at + LANES, consumers)) for at in range(0, consumers, LANES)
    ]

    def first_sweep(g, carry):
        base = partner(g) * own
        nu_load(g).wait()
        local = pltpu.roll(weights, lax.rem(LANES - base, LANES), 1)
        for i in range(own):
            weight = local[:, i : i + 1]
            known = raised_tastes(x_ref[base + i], nu_ref[g - 1, i])
            held[i, :, mine : mine + consumers] = known
            for chunk in near_chunks:
                first_ref[i : i + 1, chunk] = 1.0 + jnp.sum(
                    weight * known[:, chunk], axis=0, keepdims=True
                )
        first_ref[...] = 1.0 / first_ref[...]
        part = jnp.zeros((8, LANES), jnp.float32)
        for i in range(own):
            column = None
            for chunk in near_chunks:
                term = (
                    held[i, :, mine + chunk.start : mine + chunk.stop]
                    * first_ref[i : i + 1, chunk]
                )
                column = term if column is None else column + term
            part = placed(part, jnp.sum(column, axis=1, keepdims=True), i)
        part_slots[my_draw, partner(g)] = part
        for k in range(1, draws):
            part_copy(k, g).start()
        return carry

    lax.fori_loop(1, draws + 1, first_sweep, 0)

    for c in range(min(EARLY, pieces), pieces):
        for k in distant:
            far_copy(k, c).start()
    for hop in range(hops - 1):
        reach = 2 << hop
        wait_mkt(relay_sem.at[hop], (-reach, reach))
        signal_mkt(relay_sem.at[hop + 1], (-2 * reach, 2 * reach))

    def fill(k, c):
        far_copy(k, c).wait_recv()

        def body(i, carry):
            m = c * piece + i
            held[m, :, (k - 1) * consumers : k * consumers] = raised_tastes(
                x_ref[my_draw * own + m], far_ref[k - 1, m]
            )
            return carry

        lax.fori_loop(0, piece, body, 0, unroll=True)

    for c in range(pieces):
        for k in near:
            fill(k, c)

    product = row8
    for t in range(1, tiles):
        product = jnp.where(lane8 >= t * own, row8 + 8 * t, product)
    wide_counts = jnp.broadcast_to(counts, (slots, LANES))
    ls, means, valid = [], [], []
    for g in range(draws):
        ls.append(packed(log_share, g * own))
        means.append(packed(mean, g * own))
        valid.append(
            (product.astype(jnp.float32) < packed(wide_counts, g * own)) & (lane8 < tiles * own)
        )

    def change_of(weight, total, ls, valid):
        shares = jnp.where(valid, weight * total * inverse, 1.0)
        return jnp.where(valid, ls - jnp.log(shares), 0.0)

    def choose(values):
        chosen = values[0]
        for g in range(1, draws):
            chosen = jnp.where(my_draw == g, values[g], chosen)
        return chosen

    def spread(target, value):
        for m in range(own):
            for t in range(tiles):
                target[m, 8 * t : 8 * t + 8, :] = jnp.broadcast_to(
                    value[:, t * own + m : t * own + m + 1], (8, LANES)
                )

    spread(ls_ref, choose(ls))
    spread(mean_ref, choose(means))

    start_weights = [jnp.where(valid[g], jnp.exp(means[g]), 0.0) for g in range(draws)]
    for g in range(1, draws + 1):
        for k in range(1, draws):
            part_copy(k, g).wait_recv()
    changes = []
    peak = jnp.zeros((8, LANES), jnp.float32)
    for g in range(draws):
        total = part_slots[0, g]
        for d in range(1, draws):
            total = total + part_slots[d, g]
        changes.append(change_of(start_weights[g], total, ls[g], valid[g]))
        peak = jnp.maximum(peak, jnp.abs(changes[g]))
    peak_slots[0] = jnp.max(peak, axis=0, keepdims=True)

    def peak_copy(k):
        return pltpu.make_async_remote_copy(
            src_ref=peak_slots.at[0],
            dst_ref=peak_slots.at[k],
            send_sem=peak_send_sem.at[k - 1],
            recv_sem=peak_recv_sem.at[k - 1],
            device_id={"mkt": lax.rem(my_mkt + k, chips)},
            device_id_type=MESH,
        )

    wait_mkt(relay_sem.at[hops - 1], (-(2 << hops - 1), 2 << hops - 1))
    for k in range(1, chips):
        peak_copy(k).start()

    spread(change_ref, choose(changes))

    for c in range(pieces):
        for k in distant:
            fill(k, c)

    def largest_of(slots_ref):
        rows = [slots_ref[n] for n in range(slots_ref.shape[0])]
        while len(rows) > 1:
            rows = [
                jnp.maximum(rows[n], rows[n + 1]) if n + 1 < len(rows) else rows[n]
                for n in range(0, len(rows), 2)
            ]
        return jnp.max(rows[0], axis=1, keepdims=True)

    def step_of(largest):
        return jnp.minimum(1.0, step_cap / (largest + epsilon))

    for k in range(1, chips):
        peak_copy(k).wait_recv()
    largest = largest_of(peak_slots)
    norms_ref[0] = largest

    lanes_of = [slice(at, at + LANES) for at in range(0, draws * consumers, LANES)]

    def count_of(m):
        return counts_ref[my_draw * own + m]

    def denominators(step):
        for m in range(own):
            mean = mean_ref[m] + step * change_ref[m]
            mean_ref[m] = mean
            weight = jnp.where(row < count_of(m), jnp.exp(mean), 0.0)
            weight_ref[m] = weight
            for n, chunk in enumerate(lanes_of):
                raised = weight * held[m, :, chunk]
                total = raised[0:8]
                for t in range(1, tiles):
                    total = total + raised[8 * t : 8 * t + 8]
                partial_ref[m, 8 * n : 8 * n + 8, :] = total
            total = partial_ref[m, pl.ds(0, len(lanes_of), stride=8), :]
            for t in range(1, 8):
                total = total + partial_ref[m, pl.ds(t, len(lanes_of), stride=8), :]
            inverse_ref[m] = 1.0 / (1.0 + total)

    def sweep(step):
        denominators(step)
        peak = jnp.zeros((8, LANES), jnp.float32)
        for m in range(own):
            column = None
            for n, chunk in enumerate(lanes_of):
                term = held[m, :, chunk] * inverse_ref[m, n : n + 1, :]
                column = term if column is None else column + term
            total = jnp.sum(column, axis=1, keepdims=True)
            change = change_of(weight_ref[m], total, ls_ref[m], row < count_of(m))
            change_ref[m] = change
            for t in range(tiles):
                peak = jnp.maximum(peak, jnp.abs(change[8 * t : 8 * t + 8]))
        return jnp.max(peak, axis=0, keepdims=True)

    def gathered(source):
        tile = jnp.zeros((8, LANES), jnp.float32)
        for m in range(own):
            tile = placed(tile, source[m], m)
        return tile

    others = [(m, d) for m in range(chips) for d in range(draws) if m or d]

    def peaks_copy(it, n):
        m, d = others[n]
        return pltpu.make_async_remote_copy(
            src_ref=peaks_slots.at[it, 0],
            dst_ref=peaks_slots.at[it, n + 1],
            send_sem=peaks_send_sem.at[it],
            recv_sem=peaks_recv_sem.at[it],
            device_id={
                "mkt": lax.rem(my_mkt + m, chips),
                "draw": lax.rem(my_draw + d, draws),
            },
            device_id_type=MESH,
        )

    def peaks_all(it, sem):
        span = peaks_slots.at[it, pl.ds(1, len(others))]
        return pltpu.make_async_copy(span, span, sem.at[it])

    def mean_copy(k):
        return pltpu.make_async_remote_copy(
            src_ref=mean_slots.at[my_draw],
            dst_ref=mean_slots.at[my_draw],
            send_sem=mean_send_sem.at[k - 1],
            recv_sem=mean_recv_sem.at[k - 1],
            device_id={"draw": lax.rem(my_draw + k, draws)},
            device_id_type=MESH,
        )

    def iteration(it, step):
        peaks_slots[it, 0] = sweep(step)
        for n in range(len(others)):
            peaks_copy(it, n).start()

        @pl.when(it == ITERS - 2)
        def _():
            mean_slots[my_draw, 0] = gathered(mean_ref)
            mean_slots[my_draw, 1] = gathered(change_ref)
            for k in range(1, draws):
                mean_copy(k).start()
            for k in range(1, draws):
                for c in range(pieces):
                    far_copy(k, c).wait_send()
                for g in range(1, draws + 1):
                    part_copy(k, g).wait_send()
            for k in range(1, chips):
                peak_copy(k).wait_send()

        peaks_all(it, peaks_recv_sem).wait()
        largest = largest_of(peaks_slots.at[it])
        norms_ref[it + 1] = largest
        return step_of(largest)

    step = lax.fori_loop(0, ITERS - 1, iteration, step_of(largest))

    spot = lax.broadcasted_iota(jnp.int32, (1, ITERS), 1)
    norms = jnp.zeros((1, ITERS), jnp.float32)
    for it in range(ITERS):
        norms = jnp.where(spot == it, norms_ref[it], norms)
    norms_out[...] = norms
    for k in range(1, draws):
        mean_copy(k).wait_recv()
    mean_tiles = [mean_slots[d, 0] + step * mean_slots[d, 1] for d in range(draws)]
    for t in range(tiles):
        total = mean_tiles[0]
        total = pltpu.roll(total, LANES - t * own, 1) if t else total
        for d in range(1, draws):
            shift = (d - t) * own % LANES
            moved = pltpu.roll(mean_tiles[d], shift, 1) if shift else mean_tiles[d]
            total = jnp.where(lane8 >= d * own, moved, total)
        square[8 * t : 8 * t + 8, :] = total
    mean_rows = square[...].T
    mean_out[...] = mean_rows[0:markets, 0:slots]
    rows_ref[...] = jnp.exp(mean_rows[0:markets])

    eye = jnp.where(row == lane, 1.0, 0.0)
    ones = jnp.ones((8, draws * consumers), jnp.float32)
    scale = jnp.where(lane < slots, 0.5, 1.0)

    denominators(step)

    def last_sweep(b, carry):
        sums = []
        for u in range(block):
            chance = jnp.concatenate(
                [
                    held[b * block + u, :, chunk] * inverse_ref[b * block + u, n : n + 1, :]
                    for n, chunk in enumerate(lanes_of)
                ],
                axis=1,
            )
            low = chance - rounded(chance)
            left = jnp.concatenate([chance, low], axis=0).astype(jnp.bfloat16)
            right = jnp.concatenate([chance, ones], axis=0).astype(jnp.bfloat16)
            products = lax.dot_general(
                left, right, (((1,), (1,)), ((), ())), preferred_element_type=jnp.float32
            )
            products = jnp.concatenate(
                [products, jnp.zeros((2 * slots, LANES - slots - 8), jnp.float32)], axis=1
            )
            sums.append(scale * products[0:slots] + products[slots:])
        for at in range(0, block, 2):
            pair = sums[at]
            if at + 1 < block:
                pair = jnp.where(lane < half, pair, pltpu.roll(sums[at + 1], half, 1))
            turn[b, at // 2 * half : at // 2 * half + slots, :] = pair
        turn[b] = turn[b].T
        for u in range(block):
            other = turn[b, u % 2 * half : u % 2 * half + slots, :]
            other = pltpu.roll(other, half, 1) if u // 2 else other
            m = b * block + u
            count = counts_ref[my_draw * own + m]
            here = (row < count) & (lane < count)
            ratio = (sums[u] + other) * rows_ref[pl.ds(my_draw * own + m, 1), :]
            ratio = ratio * (1.0 / sums[u][:, slots : slots + 1])
            jac_out[m] = jnp.where(here, eye - ratio, 0.0)[:, 0:slots]
        return carry

    for b in range(own // block):
        last_sweep(b, 0)

    for k in range(1, draws):
        mean_copy(k).wait_send()
    for it in range(ITERS - 1):
        peaks_all(it, peaks_send_sem).wait()


def store(mean, jac, norms, mean_out, jac_out, norms_out, sem):
    copies = [
        pltpu.make_async_copy(source, target, sem.at[n])
        for n, (source, target) in enumerate(
            ((jac, jac_out), (mean, mean_out), (norms, norms_out))
        )
    ]
    for copy in copies:
        copy.start()
    for copy in copies:
        copy.wait()


def shards(x_char, nu_draws, coef_sigma, log_share, counts):
    markets, slots, coefs = x_char.shape
    consumers = nu_draws.shape[2]
    draws, chips = lax.axis_size("draw"), lax.axis_size("mkt")
    own = markets // draws
    pieces = divisor_up_to(own, PIECES)
    vmem = pl.BlockSpec(memory_space=pltpu.VMEM)
    f32 = jnp.float32
    dma = pltpu.SemaphoreType.DMA
    results = pl.pallas_call(
        functools.partial(kernel, draws, chips, 1.0 / (consumers * draws)),
        out_shape=(
            jax.ShapeDtypeStruct((markets, slots), f32),
            jax.ShapeDtypeStruct((own, slots, slots), f32),
            jax.ShapeDtypeStruct((1, ITERS), f32),
        ),
        in_specs=[pl.BlockSpec(memory_space=pltpu.HBM)] * 6,
        out_specs=(vmem, vmem, vmem),
        scratch_shapes=[
            pltpu.SMEM((coefs,), f32),
            pltpu.SMEM((markets,), jnp.int32),
            pltpu.VMEM((1, markets), jnp.int32),
            pltpu.VMEM((markets, slots), f32),
            pltpu.VMEM((markets, coefs, slots), f32),
            pltpu.VMEM((draws, own, coefs, consumers), f32),
            pltpu.VMEM((draws - 1, own, coefs, consumers), f32),
            pltpu.VMEM((own, slots, draws * consumers), f32),
            pltpu.VMEM((own, consumers), f32),
            pltpu.VMEM((own, draws * consumers // LANES, LANES), f32),
            pltpu.VMEM((own, draws * consumers // LANES * 8, LANES), f32),
            pltpu.VMEM((own, slots, LANES), f32),
            pltpu.VMEM((own, slots, LANES), f32),
            pltpu.VMEM((own, slots, LANES), f32),
            pltpu.VMEM((own, slots, LANES), f32),
            pltpu.VMEM((markets, LANES), f32),
            pltpu.VMEM((LANES, LANES), f32),
            pltpu.VMEM((own // divisor_up_to(own, BLOCK), LANES, LANES), f32),
            pltpu.VMEM((ITERS, 1, 1), f32),
            pltpu.VMEM((draws, draws, 8, LANES), f32),
            pltpu.VMEM((chips, 1, LANES), f32),
            pltpu.VMEM((ITERS - 1, chips * draws, 1, LANES), f32),
            pltpu.VMEM((draws, 2, 8, LANES), f32),
            dma((draws - 1, draws)),
            dma((draws - 1, draws)),
            dma((chips,)),
            dma((chips,)),
            dma((ITERS - 1,)),
            dma((ITERS - 1,)),
            dma((draws - 1, pieces)),
            dma((draws - 1, pieces)),
            dma((draws,)),
            dma((draws,)),
            pltpu.SemaphoreType.REGULAR((max(1, (chips - 1).bit_length() - 1),)),
            dma((5,)),
            dma((draws,)),
        ],
        compiler_params=pltpu.CompilerParams(
            collective_id=0, has_side_effects=True, vmem_limit_bytes=VMEM_LIMIT
        ),
        name="contraction",
    )(
        *(
            pltpu.with_memory_space_constraint(operand, pltpu.HBM)
            for operand in (
                coef_sigma,
                counts,
                counts[None, :],
                log_share,
                jnp.swapaxes(x_char, 1, 2),
                nu_draws,
            )
        )
    )
    hbm = pl.BlockSpec(memory_space=pltpu.HBM)
    mean, jac, norms = pl.pallas_call(
        store,
        out_shape=tuple(jax.ShapeDtypeStruct(r.shape, r.dtype) for r in results),
        in_specs=[vmem, vmem, vmem],
        out_specs=(hbm, hbm, hbm),
        scratch_shapes=[dma((3,))],
        name="store",
    )(*(pltpu.with_memory_space_constraint(r, pltpu.VMEM) for r in results))
    return mean, jac, norms[0]


def solution(mesh):
    return jax.shard_map(
        shards,
        mesh=mesh,
        in_specs=(P("mkt", None, None), P("mkt", None, "draw"), P(), P("mkt", None), P("mkt")),
        out_specs=(P("mkt", None), P(("mkt", "draw"), None, None), P()),
        check_vma=False,
    )
```

```python
import functools
import math

import jax
import jax.numpy as jnp
from jax import lax
from jax.experimental import pallas as pl
from jax.experimental.pallas import tpu as pltpu
from jax.sharding import PartitionSpec as P

ITERS = 3
LANES = 128
BLOCK = 4
FIRST = 4
FINAL = 6
VMEM_LIMIT = 48 * 1024 * 1024
MESH = pl.DeviceIdType.MESH

step_cap = 0.25
epsilon = 1e-06


def divisor_up_to(count, most):
    return max(size for size in range(1, most + 1) if count % size == 0)


def rounded(value):
    return value.astype(jnp.bfloat16).astype(jnp.float32)


def split2(value):
    first = rounded(value)
    return first, value - first


def kernel(
    draws,
    chips,
    inverse,
    sigma_hbm,
    counts_hbm,
    counts_row_hbm,
    log_share_hbm,
    x_hbm,
    nu_hbm,
    mean_out,
    jac_out,
    norms_out,
    sigma_ref,
    counts_ref,
    counts_row_ref,
    log_share_ref,
    x_ref,
    nu_ref,
    far_ref,
    held,
    first_ref,
    inverse_ref,
    partial_ref,
    ls_ref,
    mean_ref,
    change_ref,
    weight_ref,
    rows_ref,
    square,
    turn,
    norms_ref,
    part_slots,
    peak_slots,
    peaks_slots,
    mean_slots,
    part_send_sem,
    part_recv_sem,
    peak_send_sem,
    peak_recv_sem,
    peaks_send_sem,
    peaks_recv_sem,
    far_send_sem,
    far_recv_sem,
    mean_send_sem,
    mean_recv_sem,
    relay_sem,
    load_sem,
    nu_sem,
):
    markets, coefs, slots = x_ref.shape
    own = markets // draws
    consumers = nu_ref.shape[3]
    tiles = slots // 8
    half = LANES // 2
    block = divisor_up_to(own, BLOCK)
    pieces = far_send_sem.shape[1]
    cuts = [0, max(1, own // FIRST), max(1, own - own // FINAL), own]
    my_draw = lax.axis_index("draw")
    my_mkt = lax.axis_index("mkt")
    cores = 2 if draws % 2 == 0 else 1

    def partner(k):
        chip = (my_draw // cores + (k - 1) // cores + 1) % (draws // cores)
        core = (my_draw + k) % cores
        return chip * cores + core

    loads = [
        pltpu.make_async_copy(source, target, load_sem.at[n])
        for n, (source, target) in enumerate(
            (
                (counts_row_hbm, counts_row_ref),
                (log_share_hbm, log_share_ref),
                (sigma_hbm, sigma_ref),
                (counts_hbm, counts_ref),
                (x_hbm, x_ref),
            )
        )
    ]

    def nu_load(k):
        return pltpu.make_async_copy(
            nu_hbm.at[pl.ds(partner(k) * own, own)], nu_ref.at[k - 1], nu_sem.at[k - 1]
        )

    barrier = pltpu.get_barrier_semaphore()
    for k in range(1, draws):
        pl.semaphore_signal(
            barrier, inc=1, device_id={"draw": lax.rem(my_draw + k, draws)}, device_id_type=MESH
        )

    def beside(k):
        return (my_mkt + k >= 0) & (my_mkt + k < chips)

    def signal_mkt(sem, spans):
        for k in spans:

            @pl.when(beside(k))
            def _(k=k):
                pl.semaphore_signal(
                    sem, inc=1, device_id={"mkt": my_mkt + k}, device_id_type=MESH
                )

    def wait_mkt(sem, spans, more=0):
        count = more
        for k in spans:
            count = count + jnp.where(beside(k), 1, 0)
        pl.semaphore_wait(sem, count)

    spans = [k for k in (-2, -1, 1, 2) if abs(k) < chips]
    for load in loads:
        load.start()
    for k in range(1, draws + 1):
        nu_load(k).start()
    signal_mkt(barrier, spans)

    def far_copy(k, c):
        at, count = span_of(k, c)
        return pltpu.make_async_remote_copy(
            src_ref=nu_hbm.at[pl.ds(partner(k) * own + at, count)],
            dst_ref=far_ref.at[k - 1, pl.ds(at, count)],
            send_sem=far_send_sem.at[k - 1, c],
            recv_sem=far_recv_sem.at[k - 1, c],
            device_id={"draw": partner(k)},
            device_id_type=MESH,
        )

    near = range(max(1, draws - cores + 1), draws)
    distant = range(1, max(1, draws - cores + 1))
    parts_of = [c for c in range(pieces) if cuts[c + 1] > cuts[c]]
    far_parts = [(k, c) for c in parts_of for k in distant]
    early_parts = [(k, c) for k, c in far_parts if c == 0]
    late_parts = [(k, c) for k, c in far_parts if c > 0]
    near_parts = [(k, 0) for k in near]

    def span_of(k, c):
        return (0, own) if k in near else (cuts[c], cuts[c + 1] - cuts[c])

    lane = lax.broadcasted_iota(jnp.int32, (slots, LANES), 1)
    row = lax.broadcasted_iota(jnp.int32, (slots, LANES), 0)
    lane8 = lax.broadcasted_iota(jnp.int32, (8, LANES), 1)
    row8 = lax.broadcasted_iota(jnp.int32, (8, LANES), 0)

    wait_mkt(barrier, spans, draws - 1)
    for k, c in early_parts + near_parts:
        far_copy(k, c).start()
    hops = relay_sem.shape[0]
    signal_mkt(relay_sem.at[0], (-2, 2))

    square[...] = jnp.zeros_like(square)
    for load in loads:
        load.wait()
    square[0:markets, 0:slots] = log_share_ref[...]
    log_share = square[...].T[0:slots, :]
    square[0:1, 0:markets] = counts_row_ref[...].astype(jnp.float32)
    counts = square[0:1, :]
    usable = (row.astype(jnp.float32) < counts) & (lane < markets)
    inside = jnp.sum(jnp.where(usable, jnp.exp(log_share), 0.0), axis=0, keepdims=True)
    mean = jnp.where(usable, log_share - jnp.log(1.0 - inside), 0.0)
    weights = jnp.where(usable, jnp.exp(mean), 0.0)

    coef_row = lax.broadcasted_iota(jnp.int32, (coefs, slots), 0)
    sigma = jnp.zeros((coefs, slots), jnp.float32)
    for k in range(coefs):
        sigma = jnp.where(coef_row == k, sigma_ref[k] * math.log2(math.e), sigma)

    def raised_tastes(chars, draw):
        s1, s2 = split2(chars * sigma)
        n1, n2 = split2(draw)
        left = jnp.concatenate([s1, s1, s2, s2], axis=0).astype(jnp.bfloat16)
        right = jnp.concatenate([n1, n2, n1, n2], axis=0).astype(jnp.bfloat16)
        tastes = lax.dot_general(
            left, right, (((0,), (0,)), ((), ())), preferred_element_type=jnp.float32
        )
        return jnp.exp2(tastes)

    def packed(value, base):
        total = jnp.zeros((8, LANES), jnp.float32)
        for t in range(tiles):
            shift = (t * own - base) % LANES
            moved = value[8 * t : 8 * t + 8]
            moved = pltpu.roll(moved, shift, 1) if shift else moved
            total = jnp.where((lane8 >= t * own) & (lane8 < (t + 1) * own), moved, total)
        return total

    def placed(part, column, i):
        for t in range(tiles):
            part = jnp.where(lane8 == t * own + i, column[8 * t : 8 * t + 8], part)
        return part

    def part_copy(k, g):
        return pltpu.make_async_remote_copy(
            src_ref=part_slots.at[my_draw, partner(g)],
            dst_ref=part_slots.at[my_draw, partner(g)],
            send_sem=part_send_sem.at[k - 1, g - 1],
            recv_sem=part_recv_sem.at[k - 1, g - 1],
            device_id={"draw": lax.rem(my_draw + k, draws)},
            device_id_type=MESH,
        )

    mine = (draws - 1) * consumers
    near_chunks = [
        slice(at, min(at + LANES, consumers)) for at in range(0, consumers, LANES)
    ]

    def first_sweep(g, carry):
        base = partner(g) * own
        nu_load(g).wait()
        local = pltpu.roll(weights, lax.rem(LANES - base, LANES), 1)
        for i in range(own):
            weight = local[:, i : i + 1]
            known = raised_tastes(x_ref[base + i], nu_ref[g - 1, i])
            held[i, :, mine : mine + consumers] = known
            for chunk in near_chunks:
                first_ref[i : i + 1, chunk] = 1.0 + jnp.sum(
                    weight * known[:, chunk], axis=0, keepdims=True
                )
        first_ref[...] = 1.0 / first_ref[...]
        part = jnp.zeros((8, LANES), jnp.float32)
        for i in range(own):
            column = None
            for chunk in near_chunks:
                term = (
                    held[i, :, mine + chunk.start : mine + chunk.stop]
                    * first_ref[i : i + 1, chunk]
                )
                column = term if column is None else column + term
            part = placed(part, jnp.sum(column, axis=1, keepdims=True), i)
        part_slots[my_draw, partner(g)] = part
        for k in range(1, draws):
            part_copy(k, g).start()
        return carry

    lax.fori_loop(1, draws + 1, first_sweep, 0)

    for k, c in late_parts:
        far_copy(k, c).start()
    for hop in range(hops - 1):
        reach = 2 << hop
        wait_mkt(relay_sem.at[hop], (-reach, reach))
        signal_mkt(relay_sem.at[hop + 1], (-2 * reach, 2 * reach))

    def fill(k, c):
        far_copy(k, c).wait_recv()
        at, count = span_of(k, c)

        def body(i, carry):
            m = at + i
            held[m, :, (k - 1) * consumers : k * consumers] = raised_tastes(
                x_ref[my_draw * own + m], far_ref[k - 1, m]
            )
            return carry

        lax.fori_loop(0, count, body, 0, unroll=True)

    for k, c in near_parts:
        fill(k, c)

    product = row8
    for t in range(1, tiles):
        product = jnp.where(lane8 >= t * own, row8 + 8 * t, product)
    wide_counts = jnp.broadcast_to(counts, (slots, LANES))
    ls, means, valid = [], [], []
    for g in range(draws):
        ls.append(packed(log_share, g * own))
        means.append(packed(mean, g * own))
        valid.append(
            (product.astype(jnp.float32) < packed(wide_counts, g * own)) & (lane8 < tiles * own)
        )

    def change_of(weight, total, ls, valid):
        shares = jnp.where(valid, weight * total * inverse, 1.0)
        return jnp.where(valid, ls - jnp.log(shares), 0.0)

    def choose(values):
        chosen = values[0]
        for g in range(1, draws):
            chosen = jnp.where(my_draw == g, values[g], chosen)
        return chosen

    def spread(target, value):
        for m in range(own):
            for t in range(tiles):
                target[m, 8 * t : 8 * t + 8, :] = jnp.broadcast_to(
                    value[:, t * own + m : t * own + m + 1], (8, LANES)
                )

    spread(ls_ref, choose(ls))
    spread(mean_ref, choose(means))

    start_weights = [jnp.where(valid[g], jnp.exp(means[g]), 0.0) for g in range(draws)]
    for g in range(1, draws + 1):
        for k in range(1, draws):
            part_copy(k, g).wait_recv()
    changes = []
    peak = jnp.zeros((8, LANES), jnp.float32)
    for g in range(draws):
        total = part_slots[0, g]
        for d in range(1, draws):
            total = total + part_slots[d, g]
        changes.append(change_of(start_weights[g], total, ls[g], valid[g]))
        peak = jnp.maximum(peak, jnp.abs(changes[g]))
    peak_slots[0] = jnp.max(peak, axis=0, keepdims=True)

    def peak_copy(k):
        return pltpu.make_async_remote_copy(
            src_ref=peak_slots.at[0],
            dst_ref=peak_slots.at[k],
            send_sem=peak_send_sem.at[k - 1],
            recv_sem=peak_recv_sem.at[k - 1],
            device_id={"mkt": lax.rem(my_mkt + k, chips)},
            device_id_type=MESH,
        )

    wait_mkt(relay_sem.at[hops - 1], (-(2 << hops - 1), 2 << hops - 1))
    for k in range(1, chips):
        peak_copy(k).start()

    spread(change_ref, choose(changes))

    for k, c in far_parts:
        fill(k, c)

    def largest_of(slots_ref):
        rows = [slots_ref[n] for n in range(slots_ref.shape[0])]
        while len(rows) > 1:
            rows = [
                jnp.maximum(rows[n], rows[n + 1]) if n + 1 < len(rows) else rows[n]
                for n in range(0, len(rows), 2)
            ]
        return jnp.max(rows[0], axis=1, keepdims=True)

    def step_of(largest):
        return jnp.minimum(1.0, step_cap / (largest + epsilon))

    for k in range(1, chips):
        peak_copy(k).wait_recv()
    largest = largest_of(peak_slots)
    norms_ref[0] = largest

    lanes_of = [slice(at, at + LANES) for at in range(0, draws * consumers, LANES)]

    def count_of(m):
        return counts_ref[my_draw * own + m]

    def denominators(step):
        for m in range(own):
            mean = mean_ref[m] + step * change_ref[m]
            mean_ref[m] = mean
            weight = jnp.where(row < count_of(m), jnp.exp(mean), 0.0)
            weight_ref[m] = weight
            for n, chunk in enumerate(lanes_of):
                raised = weight * held[m, :, chunk]
                total = raised[0:8]
                for t in range(1, tiles):
                    total = total + raised[8 * t : 8 * t + 8]
                partial_ref[m, 8 * n : 8 * n + 8, :] = total
            total = partial_ref[m, pl.ds(0, len(lanes_of), stride=8), :]
            for t in range(1, 8):
                total = total + partial_ref[m, pl.ds(t, len(lanes_of), stride=8), :]
            inverse_ref[m] = 1.0 / (1.0 + total)

    def sweep(step):
        denominators(step)
        peak = jnp.zeros((8, LANES), jnp.float32)
        for m in range(own):
            column = None
            for n, chunk in enumerate(lanes_of):
                term = held[m, :, chunk] * inverse_ref[m, n : n + 1, :]
                column = term if column is None else column + term
            total = jnp.sum(column, axis=1, keepdims=True)
            change = change_of(weight_ref[m], total, ls_ref[m], row < count_of(m))
            change_ref[m] = change
            for t in range(tiles):
                peak = jnp.maximum(peak, jnp.abs(change[8 * t : 8 * t + 8]))
        return jnp.max(peak, axis=0, keepdims=True)

    def gathered(source):
        tile = jnp.zeros((8, LANES), jnp.float32)
        for m in range(own):
            tile = placed(tile, source[m], m)
        return tile

    others = [(m, d) for m in range(chips) for d in range(draws) if m or d]

    def peaks_copy(it, n):
        m, d = others[n]
        return pltpu.make_async_remote_copy(
            src_ref=peaks_slots.at[it, 0],
            dst_ref=peaks_slots.at[it, n + 1],
            send_sem=peaks_send_sem.at[it],
            recv_sem=peaks_recv_sem.at[it],
            device_id={
                "mkt": lax.rem(my_mkt + m, chips),
                "draw": lax.rem(my_draw + d, draws),
            },
            device_id_type=MESH,
        )

    def peaks_all(it, sem):
        span = peaks_slots.at[it, pl.ds(1, len(others))]
        return pltpu.make_async_copy(span, span, sem.at[it])

    def mean_copy(k):
        return pltpu.make_async_remote_copy(
            src_ref=mean_slots.at[my_draw],
            dst_ref=mean_slots.at[my_draw],
            send_sem=mean_send_sem.at[k - 1],
            recv_sem=mean_recv_sem.at[k - 1],
            device_id={"draw": lax.rem(my_draw + k, draws)},
            device_id_type=MESH,
        )

    def iteration(it, step):
        peaks_slots[it, 0] = sweep(step)
        for n in range(len(others)):
            peaks_copy(it, n).start()

        @pl.when(it == ITERS - 2)
        def _():
            mean_slots[my_draw, 0] = gathered(mean_ref)
            mean_slots[my_draw, 1] = gathered(change_ref)
            for k in range(1, draws):
                mean_copy(k).start()
            for k, c in far_parts + near_parts:
                far_copy(k, c).wait_send()
            for k in range(1, draws):
                for g in range(1, draws + 1):
                    part_copy(k, g).wait_send()
            for k in range(1, chips):
                peak_copy(k).wait_send()

        peaks_all(it, peaks_recv_sem).wait()
        largest = largest_of(peaks_slots.at[it])
        norms_ref[it + 1] = largest
        return step_of(largest)

    step = lax.fori_loop(0, ITERS - 1, iteration, step_of(largest))

    spot = lax.broadcasted_iota(jnp.int32, (1, ITERS), 1)
    norms = jnp.zeros((1, ITERS), jnp.float32)
    for it in range(ITERS):
        norms = jnp.where(spot == it, norms_ref[it], norms)
    norms_out[...] = norms
    for k in range(1, draws):
        mean_copy(k).wait_recv()
    mean_tiles = [mean_slots[d, 0] + step * mean_slots[d, 1] for d in range(draws)]
    for t in range(tiles):
        total = mean_tiles[0]
        total = pltpu.roll(total, LANES - t * own, 1) if t else total
        for d in range(1, draws):
            shift = (d - t) * own % LANES
            moved = pltpu.roll(mean_tiles[d], shift, 1) if shift else mean_tiles[d]
            total = jnp.where(lane8 >= d * own, moved, total)
        square[8 * t : 8 * t + 8, :] = total
    mean_rows = square[...].T
    mean_out[...] = mean_rows[0:markets, 0:slots]
    rows_ref[...] = jnp.exp(mean_rows[0:markets])

    eye = jnp.where(row == lane, 1.0, 0.0)
    ones = jnp.ones((8, draws * consumers), jnp.float32)
    scale = jnp.where(lane < slots, 0.5, 1.0)

    denominators(step)

    def last_sweep(b, carry):
        sums = []
        for u in range(block):
            chance = jnp.concatenate(
                [
                    held[b * block + u, :, chunk] * inverse_ref[b * block + u, n : n + 1, :]
                    for n, chunk in enumerate(lanes_of)
                ],
                axis=1,
            )
            low = chance - rounded(chance)
            left = jnp.concatenate([chance, low], axis=0).astype(jnp.bfloat16)
            right = jnp.concatenate([chance, ones], axis=0).astype(jnp.bfloat16)
            products = lax.dot_general(
                left, right, (((1,), (1,)), ((), ())), preferred_element_type=jnp.float32
            )
            products = jnp.concatenate(
                [products, jnp.zeros((2 * slots, LANES - slots - 8), jnp.float32)], axis=1
            )
            sums.append(scale * products[0:slots] + products[slots:])
        for at in range(0, block, 2):
            pair = sums[at]
            if at + 1 < block:
                pair = jnp.where(lane < half, pair, pltpu.roll(sums[at + 1], half, 1))
            turn[b, at // 2 * half : at // 2 * half + slots, :] = pair
        turn[b] = turn[b].T
        for u in range(block):
            other = turn[b, u % 2 * half : u % 2 * half + slots, :]
            other = pltpu.roll(other, half, 1) if u // 2 else other
            m = b * block + u
            count = counts_ref[my_draw * own + m]
            here = (row < count) & (lane < count)
            ratio = (sums[u] + other) * rows_ref[pl.ds(my_draw * own + m, 1), :]
            ratio = ratio * (1.0 / sums[u][:, slots : slots + 1])
            jac_out[m] = jnp.where(here, eye - ratio, 0.0)[:, 0:slots]
        return carry

    for b in range(own // block):
        last_sweep(b, 0)

    for k in range(1, draws):
        mean_copy(k).wait_send()
    for it in range(ITERS - 1):
        peaks_all(it, peaks_send_sem).wait()


def store(mean, jac, norms, mean_out, jac_out, norms_out, sem):
    copies = [
        pltpu.make_async_copy(source, target, sem.at[n])
        for n, (source, target) in enumerate(
            ((jac, jac_out), (mean, mean_out), (norms, norms_out))
        )
    ]
    for copy in copies:
        copy.start()
    for copy in copies:
        copy.wait()


def shards(x_char, nu_draws, coef_sigma, log_share, counts):
    markets, slots, coefs = x_char.shape
    consumers = nu_draws.shape[2]
    draws, chips = lax.axis_size("draw"), lax.axis_size("mkt")
    own = markets // draws
    vmem = pl.BlockSpec(memory_space=pltpu.VMEM)
    f32 = jnp.float32
    dma = pltpu.SemaphoreType.DMA
    results = pl.pallas_call(
        functools.partial(kernel, draws, chips, 1.0 / (consumers * draws)),
        out_shape=(
            jax.ShapeDtypeStruct((markets, slots), f32),
            jax.ShapeDtypeStruct((own, slots, slots), f32),
            jax.ShapeDtypeStruct((1, ITERS), f32),
        ),
        in_specs=[pl.BlockSpec(memory_space=pltpu.HBM)] * 6,
        out_specs=(vmem, vmem, vmem),
        scratch_shapes=[
            pltpu.SMEM((coefs,), f32),
            pltpu.SMEM((markets,), jnp.int32),
            pltpu.VMEM((1, markets), jnp.int32),
            pltpu.VMEM((markets, slots), f32),
            pltpu.VMEM((markets, coefs, slots), f32),
            pltpu.VMEM((draws, own, coefs, consumers), f32),
            pltpu.VMEM((draws - 1, own, coefs, consumers), f32),
            pltpu.VMEM((own, slots, draws * consumers), f32),
            pltpu.VMEM((own, consumers), f32),
            pltpu.VMEM((own, draws * consumers // LANES, LANES), f32),
            pltpu.VMEM((own, draws * consumers // LANES * 8, LANES), f32),
            pltpu.VMEM((own, slots, LANES), f32),
            pltpu.VMEM((own, slots, LANES), f32),
            pltpu.VMEM((own, slots, LANES), f32),
            pltpu.VMEM((own, slots, LANES), f32),
            pltpu.VMEM((markets, LANES), f32),
            pltpu.VMEM((LANES, LANES), f32),
            pltpu.VMEM((own // divisor_up_to(own, BLOCK), LANES, LANES), f32),
            pltpu.VMEM((ITERS, 1, 1), f32),
            pltpu.VMEM((draws, draws, 8, LANES), f32),
            pltpu.VMEM((chips, 1, LANES), f32),
            pltpu.VMEM((ITERS - 1, chips * draws, 1, LANES), f32),
            pltpu.VMEM((draws, 2, 8, LANES), f32),
            dma((draws - 1, draws)),
            dma((draws - 1, draws)),
            dma((chips,)),
            dma((chips,)),
            dma((ITERS - 1,)),
            dma((ITERS - 1,)),
            dma((draws - 1, 3)),
            dma((draws - 1, 3)),
            dma((draws,)),
            dma((draws,)),
            pltpu.SemaphoreType.REGULAR((max(1, (chips - 1).bit_length() - 1),)),
            dma((5,)),
            dma((draws,)),
        ],
        compiler_params=pltpu.CompilerParams(
            collective_id=0, has_side_effects=True, vmem_limit_bytes=VMEM_LIMIT
        ),
        name="contraction",
    )(
        *(
            pltpu.with_memory_space_constraint(operand, pltpu.HBM)
            for operand in (
                coef_sigma,
                counts,
                counts[None, :],
                log_share,
                jnp.swapaxes(x_char, 1, 2),
                nu_draws,
            )
        )
    )
    hbm = pl.BlockSpec(memory_space=pltpu.HBM)
    mean, jac, norms = pl.pallas_call(
        store,
        out_shape=tuple(jax.ShapeDtypeStruct(r.shape, r.dtype) for r in results),
        in_specs=[vmem, vmem, vmem],
        out_specs=(hbm, hbm, hbm),
        scratch_shapes=[dma((3,))],
        name="store",
    )(*(pltpu.with_memory_space_constraint(r, pltpu.VMEM) for r in results))
    return mean, jac, norms[0]


def solution(mesh):
    return jax.shard_map(
        shards,
        mesh=mesh,
        in_specs=(P("mkt", None, None), P("mkt", None, "draw"), P(), P("mkt", None), P("mkt")),
        out_specs=(P("mkt", None), P(("mkt", "draw"), None, None), P()),
        check_vma=False,
    )
```

```python
import functools
import math

import jax
import jax.numpy as jnp
from jax import lax
from jax.experimental import pallas as pl
from jax.experimental.pallas import tpu as pltpu
from jax.sharding import PartitionSpec as P

ITERS = 3
LANES = 128
BLOCK = 2
FIRST = 4
FINAL = 6
VMEM_LIMIT = 48 * 1024 * 1024
MESH = pl.DeviceIdType.MESH

step_cap = 0.25
epsilon = 1e-06


def divisor_up_to(count, most):
    return max(size for size in range(1, most + 1) if count % size == 0)


def rounded(value):
    return value.astype(jnp.bfloat16).astype(jnp.float32)


def split2(value):
    first = rounded(value)
    return first, value - first


def kernel(
    draws,
    chips,
    inverse,
    sigma_hbm,
    counts_hbm,
    counts_row_hbm,
    log_share_hbm,
    x_hbm,
    nu_hbm,
    mean_out,
    jac_out,
    norms_out,
    sigma_ref,
    counts_ref,
    counts_row_ref,
    log_share_ref,
    x_ref,
    nu_ref,
    far_ref,
    held,
    first_ref,
    inverse_ref,
    partial_ref,
    ls_ref,
    mean_ref,
    change_ref,
    weight_ref,
    rows_ref,
    square,
    turn,
    norms_ref,
    part_slots,
    peak_slots,
    peaks_slots,
    mean_slots,
    part_send_sem,
    part_recv_sem,
    peak_send_sem,
    peak_recv_sem,
    peaks_send_sem,
    peaks_recv_sem,
    far_send_sem,
    far_recv_sem,
    mean_send_sem,
    mean_recv_sem,
    relay_sem,
    load_sem,
    nu_sem,
):
    markets, coefs, slots = x_ref.shape
    own = markets // draws
    consumers = nu_ref.shape[3]
    tiles = slots // 8
    half = LANES // 2
    block = divisor_up_to(own, BLOCK)
    pieces = far_send_sem.shape[1]
    cuts = [0, max(1, own // FIRST), max(1, own - own // FINAL), own]
    my_draw = lax.axis_index("draw")
    my_mkt = lax.axis_index("mkt")
    cores = 2 if draws % 2 == 0 else 1

    def partner(k):
        chip = (my_draw // cores + (k - 1) // cores + 1) % (draws // cores)
        core = (my_draw + k) % cores
        return chip * cores + core

    loads = [
        pltpu.make_async_copy(source, target, load_sem.at[n])
        for n, (source, target) in enumerate(
            (
                (counts_row_hbm, counts_row_ref),
                (log_share_hbm, log_share_ref),
                (sigma_hbm, sigma_ref),
                (counts_hbm, counts_ref),
                (x_hbm, x_ref),
            )
        )
    ]

    def nu_load(k):
        return pltpu.make_async_copy(
            nu_hbm.at[pl.ds(partner(k) * own, own)], nu_ref.at[k - 1], nu_sem.at[k - 1]
        )

    barrier = pltpu.get_barrier_semaphore()
    for k in range(1, draws):
        pl.semaphore_signal(
            barrier, inc=1, device_id={"draw": lax.rem(my_draw + k, draws)}, device_id_type=MESH
        )

    def beside(k):
        return (my_mkt + k >= 0) & (my_mkt + k < chips)

    def signal_mkt(sem, spans):
        for k in spans:

            @pl.when(beside(k))
            def _(k=k):
                pl.semaphore_signal(
                    sem, inc=1, device_id={"mkt": my_mkt + k}, device_id_type=MESH
                )

    def wait_mkt(sem, spans, more=0):
        count = more
        for k in spans:
            count = count + jnp.where(beside(k), 1, 0)
        pl.semaphore_wait(sem, count)

    spans = [k for k in (-2, -1, 1, 2) if abs(k) < chips]
    for load in loads:
        load.start()
    for k in range(1, draws + 1):
        nu_load(k).start()
    signal_mkt(barrier, spans)

    def far_copy(k, c):
        at, count = span_of(k, c)
        return pltpu.make_async_remote_copy(
            src_ref=nu_hbm.at[pl.ds(partner(k) * own + at, count)],
            dst_ref=far_ref.at[k - 1, pl.ds(at, count)],
            send_sem=far_send_sem.at[k - 1, c],
            recv_sem=far_recv_sem.at[k - 1, c],
            device_id={"draw": partner(k)},
            device_id_type=MESH,
        )

    near = range(max(1, draws - cores + 1), draws)
    distant = range(1, max(1, draws - cores + 1))
    parts_of = [c for c in range(pieces) if cuts[c + 1] > cuts[c]]
    far_parts = [(k, c) for c in parts_of for k in distant]
    early_parts = [(k, c) for k, c in far_parts if c == 0]
    late_parts = [(k, c) for k, c in far_parts if c > 0]
    near_parts = [(k, 0) for k in near]

    def span_of(k, c):
        return (0, own) if k in near else (cuts[c], cuts[c + 1] - cuts[c])

    lane = lax.broadcasted_iota(jnp.int32, (slots, LANES), 1)
    row = lax.broadcasted_iota(jnp.int32, (slots, LANES), 0)
    lane8 = lax.broadcasted_iota(jnp.int32, (8, LANES), 1)
    row8 = lax.broadcasted_iota(jnp.int32, (8, LANES), 0)

    wait_mkt(barrier, spans, draws - 1)
    for k, c in early_parts + near_parts:
        far_copy(k, c).start()
    hops = relay_sem.shape[0]
    signal_mkt(relay_sem.at[0], (-2, 2))

    square[...] = jnp.zeros_like(square)
    for load in loads:
        load.wait()
    square[0:markets, 0:slots] = log_share_ref[...]
    log_share = square[...].T[0:slots, :]
    square[0:1, 0:markets] = counts_row_ref[...].astype(jnp.float32)
    counts = square[0:1, :]
    usable = (row.astype(jnp.float32) < counts) & (lane < markets)
    inside = jnp.sum(jnp.where(usable, jnp.exp(log_share), 0.0), axis=0, keepdims=True)
    mean = jnp.where(usable, log_share - jnp.log(1.0 - inside), 0.0)
    weights = jnp.where(usable, jnp.exp(mean), 0.0)

    coef_row = lax.broadcasted_iota(jnp.int32, (coefs, slots), 0)
    sigma = jnp.zeros((coefs, slots), jnp.float32)
    for k in range(coefs):
        sigma = jnp.where(coef_row == k, sigma_ref[k] * math.log2(math.e), sigma)

    def raised_tastes(chars, draw):
        s1, s2 = split2(chars * sigma)
        n1, n2 = split2(draw)
        left = jnp.concatenate([s1, s1, s2, s2], axis=0).astype(jnp.bfloat16)
        right = jnp.concatenate([n1, n2, n1, n2], axis=0).astype(jnp.bfloat16)
        tastes = lax.dot_general(
            left, right, (((0,), (0,)), ((), ())), preferred_element_type=jnp.float32
        )
        return jnp.exp2(tastes)

    def packed(value, base):
        total = jnp.zeros((8, LANES), jnp.float32)
        for t in range(tiles):
            shift = (t * own - base) % LANES
            moved = value[8 * t : 8 * t + 8]
            moved = pltpu.roll(moved, shift, 1) if shift else moved
            total = jnp.where((lane8 >= t * own) & (lane8 < (t + 1) * own), moved, total)
        return total

    def placed(part, column, i):
        for t in range(tiles):
            part = jnp.where(lane8 == t * own + i, column[8 * t : 8 * t + 8], part)
        return part

    def part_copy(k, g):
        return pltpu.make_async_remote_copy(
            src_ref=part_slots.at[my_draw, partner(g)],
            dst_ref=part_slots.at[my_draw, partner(g)],
            send_sem=part_send_sem.at[k - 1, g - 1],
            recv_sem=part_recv_sem.at[k - 1, g - 1],
            device_id={"draw": lax.rem(my_draw + k, draws)},
            device_id_type=MESH,
        )

    mine = (draws - 1) * consumers
    near_chunks = [
        slice(at, min(at + LANES, consumers)) for at in range(0, consumers, LANES)
    ]

    def first_sweep(g, carry):
        base = partner(g) * own
        nu_load(g).wait()
        local = pltpu.roll(weights, lax.rem(LANES - base, LANES), 1)
        for i in range(own):
            weight = local[:, i : i + 1]
            known = raised_tastes(x_ref[base + i], nu_ref[g - 1, i])
            held[i, :, mine : mine + consumers] = known
            for chunk in near_chunks:
                first_ref[i : i + 1, chunk] = 1.0 + jnp.sum(
                    weight * known[:, chunk], axis=0, keepdims=True
                )
        first_ref[...] = 1.0 / first_ref[...]
        part = jnp.zeros((8, LANES), jnp.float32)
        for i in range(own):
            column = None
            for chunk in near_chunks:
                term = (
                    held[i, :, mine + chunk.start : mine + chunk.stop]
                    * first_ref[i : i + 1, chunk]
                )
                column = term if column is None else column + term
            part = placed(part, jnp.sum(column, axis=1, keepdims=True), i)
        part_slots[my_draw, partner(g)] = part
        for k in range(1, draws):
            part_copy(k, g).start()
        return carry

    lax.fori_loop(1, draws + 1, first_sweep, 0)

    for k, c in late_parts:
        far_copy(k, c).start()
    for hop in range(hops - 1):
        reach = 2 << hop
        wait_mkt(relay_sem.at[hop], (-reach, reach))
        signal_mkt(relay_sem.at[hop + 1], (-2 * reach, 2 * reach))

    def fill(k, c):
        far_copy(k, c).wait_recv()
        at, count = span_of(k, c)

        def body(i, carry):
            m = at + i
            held[m, :, (k - 1) * consumers : k * consumers] = raised_tastes(
                x_ref[my_draw * own + m], far_ref[k - 1, m]
            )
            return carry

        lax.fori_loop(0, count, body, 0, unroll=True)

    for k, c in near_parts:
        fill(k, c)

    product = row8
    for t in range(1, tiles):
        product = jnp.where(lane8 >= t * own, row8 + 8 * t, product)
    wide_counts = jnp.broadcast_to(counts, (slots, LANES))
    ls, means, valid = [], [], []
    for g in range(draws):
        ls.append(packed(log_share, g * own))
        means.append(packed(mean, g * own))
        valid.append(
            (product.astype(jnp.float32) < packed(wide_counts, g * own)) & (lane8 < tiles * own)
        )

    def change_of(weight, total, ls, valid):
        shares = jnp.where(valid, weight * total * inverse, 1.0)
        return jnp.where(valid, ls - jnp.log(shares), 0.0)

    def choose(values):
        chosen = values[0]
        for g in range(1, draws):
            chosen = jnp.where(my_draw == g, values[g], chosen)
        return chosen

    def spread(target, value):
        for m in range(own):
            for t in range(tiles):
                target[m, 8 * t : 8 * t + 8, :] = jnp.broadcast_to(
                    value[:, t * own + m : t * own + m + 1], (8, LANES)
                )

    spread(ls_ref, choose(ls))
    spread(mean_ref, choose(means))

    start_weights = [jnp.where(valid[g], jnp.exp(means[g]), 0.0) for g in range(draws)]
    for g in range(1, draws + 1):
        for k in range(1, draws):
            part_copy(k, g).wait_recv()
    changes = []
    peak = jnp.zeros((8, LANES), jnp.float32)
    for g in range(draws):
        total = part_slots[0, g]
        for d in range(1, draws):
            total = total + part_slots[d, g]
        changes.append(change_of(start_weights[g], total, ls[g], valid[g]))
        peak = jnp.maximum(peak, jnp.abs(changes[g]))
    peak_slots[0] = jnp.max(peak, axis=0, keepdims=True)

    def peak_copy(k):
        return pltpu.make_async_remote_copy(
            src_ref=peak_slots.at[0],
            dst_ref=peak_slots.at[k],
            send_sem=peak_send_sem.at[k - 1],
            recv_sem=peak_recv_sem.at[k - 1],
            device_id={"mkt": lax.rem(my_mkt + k, chips)},
            device_id_type=MESH,
        )

    wait_mkt(relay_sem.at[hops - 1], (-(2 << hops - 1), 2 << hops - 1))
    for k in range(1, chips):
        peak_copy(k).start()

    spread(change_ref, choose(changes))

    for k, c in far_parts:
        fill(k, c)

    def largest_of(slots_ref):
        rows = [slots_ref[n] for n in range(slots_ref.shape[0])]
        while len(rows) > 1:
            rows = [
                jnp.maximum(rows[n], rows[n + 1]) if n + 1 < len(rows) else rows[n]
                for n in range(0, len(rows), 2)
            ]
        return jnp.max(rows[0], axis=1, keepdims=True)

    def step_of(largest):
        return jnp.minimum(1.0, step_cap / (largest + epsilon))

    for k in range(1, chips):
        peak_copy(k).wait_recv()
    largest = largest_of(peak_slots)
    norms_ref[0] = largest

    lanes_of = [slice(at, at + LANES) for at in range(0, draws * consumers, LANES)]

    def count_of(m):
        return counts_ref[my_draw * own + m]

    def denominators(step):
        for m in range(own):
            mean = mean_ref[m] + step * change_ref[m]
            mean_ref[m] = mean
            weight = jnp.where(row < count_of(m), jnp.exp(mean), 0.0)
            weight_ref[m] = weight
            for n, chunk in enumerate(lanes_of):
                raised = weight * held[m, :, chunk]
                total = raised[0:8]
                for t in range(1, tiles):
                    total = total + raised[8 * t : 8 * t + 8]
                partial_ref[m, 8 * n : 8 * n + 8, :] = total
            total = partial_ref[m, pl.ds(0, len(lanes_of), stride=8), :]
            for t in range(1, 8):
                total = total + partial_ref[m, pl.ds(t, len(lanes_of), stride=8), :]
            inverse_ref[m] = 1.0 / (1.0 + total)

    def sweep(step):
        denominators(step)
        peak = jnp.zeros((8, LANES), jnp.float32)
        for m in range(own):
            column = None
            for n, chunk in enumerate(lanes_of):
                term = held[m, :, chunk] * inverse_ref[m, n : n + 1, :]
                column = term if column is None else column + term
            total = jnp.sum(column, axis=1, keepdims=True)
            change = change_of(weight_ref[m], total, ls_ref[m], row < count_of(m))
            change_ref[m] = change
            for t in range(tiles):
                peak = jnp.maximum(peak, jnp.abs(change[8 * t : 8 * t + 8]))
        return jnp.max(peak, axis=0, keepdims=True)

    def gathered(source):
        tile = jnp.zeros((8, LANES), jnp.float32)
        for m in range(own):
            tile = placed(tile, source[m], m)
        return tile

    others = [(m, d) for m in range(chips) for d in range(draws) if m or d]

    def peaks_copy(it, n):
        m, d = others[n]
        return pltpu.make_async_remote_copy(
            src_ref=peaks_slots.at[it, 0],
            dst_ref=peaks_slots.at[it, n + 1],
            send_sem=peaks_send_sem.at[it],
            recv_sem=peaks_recv_sem.at[it],
            device_id={
                "mkt": lax.rem(my_mkt + m, chips),
                "draw": lax.rem(my_draw + d, draws),
            },
            device_id_type=MESH,
        )

    def peaks_all(it, sem):
        span = peaks_slots.at[it, pl.ds(1, len(others))]
        return pltpu.make_async_copy(span, span, sem.at[it])

    def mean_copy(k):
        return pltpu.make_async_remote_copy(
            src_ref=mean_slots.at[my_draw],
            dst_ref=mean_slots.at[my_draw],
            send_sem=mean_send_sem.at[k - 1],
            recv_sem=mean_recv_sem.at[k - 1],
            device_id={"draw": lax.rem(my_draw + k, draws)},
            device_id_type=MESH,
        )

    def iteration(it, step):
        peaks_slots[it, 0] = sweep(step)
        for n in range(len(others)):
            peaks_copy(it, n).start()

        @pl.when(it == ITERS - 2)
        def _():
            mean_slots[my_draw, 0] = gathered(mean_ref)
            mean_slots[my_draw, 1] = gathered(change_ref)
            for k in range(1, draws):
                mean_copy(k).start()
            for k, c in far_parts + near_parts:
                far_copy(k, c).wait_send()
            for k in range(1, draws):
                for g in range(1, draws + 1):
                    part_copy(k, g).wait_send()
            for k in range(1, chips):
                peak_copy(k).wait_send()

        peaks_all(it, peaks_recv_sem).wait()
        largest = largest_of(peaks_slots.at[it])
        norms_ref[it + 1] = largest
        return step_of(largest)

    step = lax.fori_loop(0, ITERS - 1, iteration, step_of(largest))

    spot = lax.broadcasted_iota(jnp.int32, (1, ITERS), 1)
    norms = jnp.zeros((1, ITERS), jnp.float32)
    for it in range(ITERS):
        norms = jnp.where(spot == it, norms_ref[it], norms)
    norms_out[...] = norms
    for k in range(1, draws):
        mean_copy(k).wait_recv()
    mean_tiles = [mean_slots[d, 0] + step * mean_slots[d, 1] for d in range(draws)]
    for t in range(tiles):
        total = mean_tiles[0]
        total = pltpu.roll(total, LANES - t * own, 1) if t else total
        for d in range(1, draws):
            shift = (d - t) * own % LANES
            moved = pltpu.roll(mean_tiles[d], shift, 1) if shift else mean_tiles[d]
            total = jnp.where(lane8 >= d * own, moved, total)
        square[8 * t : 8 * t + 8, :] = total
    mean_rows = square[...].T
    mean_out[...] = mean_rows[0:markets, 0:slots]
    rows_ref[...] = jnp.exp(mean_rows[0:markets])

    eye = jnp.where(row == lane, 1.0, 0.0)
    ones = jnp.ones((8, draws * consumers), jnp.float32)
    scale = jnp.where(lane < slots, 0.5, 1.0)

    denominators(step)

    def last_sweep(b, carry):
        sums = []
        for u in range(block):
            chance = jnp.concatenate(
                [
                    held[b * block + u, :, chunk] * inverse_ref[b * block + u, n : n + 1, :]
                    for n, chunk in enumerate(lanes_of)
                ],
                axis=1,
            )
            low = chance - rounded(chance)
            left = jnp.concatenate([chance, low], axis=0).astype(jnp.bfloat16)
            right = jnp.concatenate([chance, ones], axis=0).astype(jnp.bfloat16)
            products = lax.dot_general(
                left, right, (((1,), (1,)), ((), ())), preferred_element_type=jnp.float32
            )
            products = jnp.concatenate(
                [products, jnp.zeros((2 * slots, LANES - slots - 8), jnp.float32)], axis=1
            )
            sums.append(scale * products[0:slots] + products[slots:])
        for at in range(0, block, 2):
            pair = sums[at]
            if at + 1 < block:
                pair = jnp.where(lane < half, pair, pltpu.roll(sums[at + 1], half, 1))
            turn[b, at // 2 * half : at // 2 * half + slots, :] = pair
        turn[b] = turn[b].T
        for u in range(block):
            other = turn[b, u % 2 * half : u % 2 * half + slots, :]
            other = pltpu.roll(other, half, 1) if u // 2 else other
            m = b * block + u
            count = counts_ref[my_draw * own + m]
            here = (row < count) & (lane < count)
            ratio = (sums[u] + other) * rows_ref[pl.ds(my_draw * own + m, 1), :]
            ratio = ratio * (1.0 / sums[u][:, slots : slots + 1])
            jac_out[m] = jnp.where(here, eye - ratio, 0.0)[:, 0:slots]
        return carry

    for b in range(own // block):
        last_sweep(b, 0)

    for k in range(1, draws):
        mean_copy(k).wait_send()
    for it in range(ITERS - 1):
        peaks_all(it, peaks_send_sem).wait()


def store(mean, jac, norms, mean_out, jac_out, norms_out, sem):
    copies = [
        pltpu.make_async_copy(source, target, sem.at[n])
        for n, (source, target) in enumerate(
            ((jac, jac_out), (mean, mean_out), (norms, norms_out))
        )
    ]
    for copy in copies:
        copy.start()
    for copy in copies:
        copy.wait()


def shards(x_char, nu_draws, coef_sigma, log_share, counts):
    markets, slots, coefs = x_char.shape
    consumers = nu_draws.shape[2]
    draws, chips = lax.axis_size("draw"), lax.axis_size("mkt")
    own = markets // draws
    vmem = pl.BlockSpec(memory_space=pltpu.VMEM)
    f32 = jnp.float32
    dma = pltpu.SemaphoreType.DMA
    results = pl.pallas_call(
        functools.partial(kernel, draws, chips, 1.0 / (consumers * draws)),
        out_shape=(
            jax.ShapeDtypeStruct((markets, slots), f32),
            jax.ShapeDtypeStruct((own, slots, slots), f32),
            jax.ShapeDtypeStruct((1, ITERS), f32),
        ),
        in_specs=[pl.BlockSpec(memory_space=pltpu.HBM)] * 6,
        out_specs=(vmem, vmem, vmem),
        scratch_shapes=[
            pltpu.SMEM((coefs,), f32),
            pltpu.SMEM((markets,), jnp.int32),
            pltpu.VMEM((1, markets), jnp.int32),
            pltpu.VMEM((markets, slots), f32),
            pltpu.VMEM((markets, coefs, slots), f32),
            pltpu.VMEM((draws, own, coefs, consumers), f32),
            pltpu.VMEM((draws - 1, own, coefs, consumers), f32),
            pltpu.VMEM((own, slots, draws * consumers), f32),
            pltpu.VMEM((own, consumers), f32),
            pltpu.VMEM((own, draws * consumers // LANES, LANES), f32),
            pltpu.VMEM((own, draws * consumers // LANES * 8, LANES), f32),
            pltpu.VMEM((own, slots, LANES), f32),
            pltpu.VMEM((own, slots, LANES), f32),
            pltpu.VMEM((own, slots, LANES), f32),
            pltpu.VMEM((own, slots, LANES), f32),
            pltpu.VMEM((markets, LANES), f32),
            pltpu.VMEM((LANES, LANES), f32),
            pltpu.VMEM((own // divisor_up_to(own, BLOCK), LANES, LANES), f32),
            pltpu.VMEM((ITERS, 1, 1), f32),
            pltpu.VMEM((draws, draws, 8, LANES), f32),
            pltpu.VMEM((chips, 1, LANES), f32),
            pltpu.VMEM((ITERS - 1, chips * draws, 1, LANES), f32),
            pltpu.VMEM((draws, 2, 8, LANES), f32),
            dma((draws - 1, draws)),
            dma((draws - 1, draws)),
            dma((chips,)),
            dma((chips,)),
            dma((ITERS - 1,)),
            dma((ITERS - 1,)),
            dma((draws - 1, 3)),
            dma((draws - 1, 3)),
            dma((draws,)),
            dma((draws,)),
            pltpu.SemaphoreType.REGULAR((max(1, (chips - 1).bit_length() - 1),)),
            dma((5,)),
            dma((draws,)),
        ],
        compiler_params=pltpu.CompilerParams(
            collective_id=0, has_side_effects=True, vmem_limit_bytes=VMEM_LIMIT
        ),
        name="contraction",
    )(
        *(
            pltpu.with_memory_space_constraint(operand, pltpu.HBM)
            for operand in (
                coef_sigma,
                counts,
                counts[None, :],
                log_share,
                jnp.swapaxes(x_char, 1, 2),
                nu_draws,
            )
        )
    )
    hbm = pl.BlockSpec(memory_space=pltpu.HBM)
    mean, jac, norms = pl.pallas_call(
        store,
        out_shape=tuple(jax.ShapeDtypeStruct(r.shape, r.dtype) for r in results),
        in_specs=[vmem, vmem, vmem],
        out_specs=(hbm, hbm, hbm),
        scratch_shapes=[dma((3,))],
        name="store",
    )(*(pltpu.with_memory_space_constraint(r, pltpu.VMEM) for r in results))
    return mean, jac, norms[0]


def solution(mesh):
    return jax.shard_map(
        shards,
        mesh=mesh,
        in_specs=(P("mkt", None, None), P("mkt", None, "draw"), P(), P("mkt", None), P("mkt")),
        out_specs=(P("mkt", None), P(("mkt", "draw"), None, None), P()),
        check_vma=False,
    )
```
